256 devices in a mesh: blk: 64 (over z, y, x_lo), pix: 4 (over x_hi, core).
Axes of the slice: x: 4 (x_hi: 2, x_lo: 2; x = x_hi * 2 + x_lo), y: 4, z: 8, core: 2. Of those that a mesh axis runs over, the one named last changes fastest.
Arguments:
- pixels: bfloat16 [262144, 224], P(('blk', 'pix')), may hold values from -6 to 6
- bundles: bfloat16 [128, 224, 64], P('blk'), may hold values from -0.375 to 0.375
- assign: int32 [262144, 1], P(('blk', 'pix')), may hold values from 0 to 127; in each aligned block of 1024 rows (0 to 1023, 1024 to 2047, ...) at most 16 rows name the same one
Outputs:
- abundances: float32 [262144, 64], P(('blk', 'pix'))
- residual_energy: float32 [64, 128], P('blk')
The draws below stay inside these ranges and needn't reach their ends.
Inputs may be any that keep to these rules, and one draw needn't show every extreme that they name: `assign`: among the 1024 rows of one device no bundle is named more than 16 times; in every draw some device names some bundle exactly 16 times; every bundle is named somewhere.
All inputs are finite; a program needn't handle non-finite values. Where the reference program divides by a largest or mean magnitude, that divisor is 1e-20 or more.
Results may differ from the reference program's by a relative error of at most 0.0003.
Values may be sent and summed in bfloat16 or wider, within the bound.
No kernel may reach another device: no remote copies, remote signals or barrier semaphores. Data moves between devices by JAX's collectives and lax.ppermute only.
A program may use at most 64 MiB of HBM per device.

```python
import math
import jax
import jax.numpy as jnp
import numpy as np
from jax import lax

BANDS = 224
ENDMEMBERS = 64
ITERS = 8
PIX_DEV = 1024
BUNDLES = 128
CAP = 16
PIXELS = 262144
N_BLK = 64
N_PIX = 4


def shard_levels(key, extent, cuts, least, largest):
    def one(dim, parts):
        heights = jax.random.uniform(jax.random.fold_in(jax.random.fold_in(key, 6), dim), (parts,), jnp.float32, least / len(cuts), largest / len(cuts))
        return jnp.repeat(jnp.exp(heights), extent[dim] // parts).reshape((-1,) + (1,) * (len(extent) - dim - 1))

    loudness = one(*cuts[0])
    for cut in cuts[1:]:
        loudness = loudness * one(*cut)
    return loudness


def routed_block(own_key, own, number, rows, amount, top, most, skew):
    ranking = jax.random.permutation(own_key, amount)
    packed, common = shares(amount, rows * top, most, skew, True), shares(amount, rows * top, most, skew, False)
    places = jnp.arange(amount)

    def named(sizes, rotation):
        used = int((sizes > 0).sum())
        fixed = max(1, used // 4)
        passed = fixed + (places - fixed + rotation * (used - fixed)) % max(1, amount - fixed)
        return jnp.zeros((amount,), jnp.int32).at[ranking[jnp.where(places < fixed, places, passed)]].set(jnp.asarray(sizes, jnp.int32))

    sizes = jnp.where(number % 4 == 0, named(packed, number // 4), named(common, number - number // 4 - 1))
    mixed = jax.random.permutation(jax.random.fold_in(own, 3), amount)
    giver, receiver = mixed[0:amount // 2 * 2:2], mixed[1:amount // 2 * 2:2]
    room = jnp.minimum(sizes[giver] - 1, most - sizes[receiver]) // 2
    room = jnp.where((giver == ranking[0]) | (receiver == ranking[0]) | (sizes[receiver] == 0), 0, jnp.maximum(room, 0))
    passed = jax.random.randint(jax.random.fold_in(own, 4), (amount // 2,), 0, 1 << 20) % (room + 1)
    sizes = sizes.at[giver].add(-passed).at[receiver].add(passed)
    members = jnp.searchsorted(jnp.cumsum(sizes), jnp.arange(rows * top), side="right").astype(jnp.int32)
    table = members.reshape(top, rows).T
    table = table[jax.random.permutation(jax.random.fold_in(own, 1), rows)]
    rotation = jax.random.randint(jax.random.fold_in(own, 2), (rows, 1), 0, top)
    return jnp.take_along_axis(table, (jnp.arange(top)[None, :] + rotation) % top, axis=1)


def shares(amount, total, reach, slope, full):
    portions = [(1 << 20) // math.isqrt(grade ** slope) + 1 for grade in range(1, amount + 1)]
    largest = reach if full else min(reach, max(-(-total // amount), total * portions[0] // sum(portions)))
    least = 1 if total - largest >= amount - 1 else 0
    counts, rest = [largest] + [least] * (amount - 1), total - largest - least * (amount - 1)
    while rest > 0:
        movable = [i for i in range(1, amount) if counts[i] < largest] or [i for i in range(1, amount) if counts[i] < reach]
        mass, budget = sum([portions[i] for i in movable]), rest
        for i in movable:
            extra = min(reach - counts[i], max(1, budget * portions[i] // mass), rest)
            counts[i] = counts[i] + extra
            rest = rest - extra
    return np.array(counts)


def normal_values(rng, extent, scale, bound, split=(), held_as=jnp.bfloat16):
    values = scale * jax.random.normal(rng, extent, jnp.float32)
    if split:
        values = values * shard_levels(rng, extent, split, -0.22, 0.18)
    return jnp.clip(values, -bound, bound).astype(held_as)


def setup_inputs(seed: int = 0) -> dict:
    key_of = jax.random.split(jax.random.key(seed), 4)
    pixels = normal_values(key_of[0], (PIXELS, BANDS), 1.0, 6.0, ((0, 256),))
    bundles = normal_values(key_of[1], (BUNDLES, BANDS, ENDMEMBERS), BANDS ** -0.5, 0.375, ((0, 64),))
    assign_keys = jax.random.split(jax.random.fold_in(key_of[2], 1), PIXELS // PIX_DEV)
    assign_turns = jax.random.permutation(jax.random.fold_in(key_of[2], 3), PIXELS // PIX_DEV)
    assign = jax.vmap(lambda own, number: routed_block(jax.random.fold_in(key_of[2], 2), own, number, PIX_DEV, BUNDLES, 1, CAP, 1))(assign_keys, assign_turns).reshape((PIXELS, 1))
    return {"pixels": pixels, "bundles": bundles, "assign": assign}


sum_weight = 0.015625


def make_slots(assign, count, cap):
    labels = assign[:, 0].astype(jnp.int32)
    onehot = (labels[:, None] == jnp.arange(count, dtype=jnp.int32)[None, :]).astype(jnp.int32)
    ranked = jnp.sum(jnp.cumsum(onehot, axis=0) * onehot, axis=1) - 1
    return (labels * cap + ranked).astype(jnp.int32)


def solve_ref(blocks, spectra, gram, step):
    wide = spectra.astype(jnp.float32)
    target = jnp.einsum("nsb,nbm->nsm", blocks.astype(jnp.float32), wide, precision=lax.Precision.HIGHEST) + sum_weight

    def sweep(index, state):
        grad = jnp.einsum("nsm,nmk->nsk", state, gram, precision=lax.Precision.HIGHEST)
        return jnp.maximum(state - step[:, None, None] * (grad - target), 0.0)

    state = lax.fori_loop(0, ITERS, sweep, jnp.zeros_like(target))
    fitted = jnp.einsum("nsm,nbm->nsb", state, wide, precision=lax.Precision.HIGHEST)
    misfit = blocks.astype(jnp.float32) - fitted
    return state, jnp.sum(misfit * misfit, axis=-1)


def reference(pixels, bundles, assign):
    wide = bundles.astype(jnp.float32)
    gram = jnp.einsum("nbm,nbk->nmk", wide, wide, precision=lax.Precision.HIGHEST) + sum_weight
    step = 1.0 / jnp.max(jnp.sum(jnp.abs(gram), axis=2), axis=1)
    scale = BANDS * PIX_DEV * N_PIX / BUNDLES
    blocks_in = pixels.reshape(N_BLK * N_PIX, PIX_DEV, BANDS)
    labels_in = assign.reshape(N_BLK * N_PIX, PIX_DEV, 1)

    def per_block(item):
        values, labels = item
        slots = make_slots(labels, BUNDLES, CAP)
        flat = jnp.zeros((BUNDLES * CAP, BANDS), jnp.bfloat16).at[slots].set(values)
        valid = jnp.zeros((BUNDLES * CAP,), jnp.float32).at[slots].set(1.0).reshape(BUNDLES, CAP)
        state, misfit = solve_ref(flat.reshape(BUNDLES, CAP, BANDS), bundles, gram, step)
        chosen = state.reshape(BUNDLES * CAP, ENDMEMBERS)[slots]
        energy = jnp.sum(misfit * valid / scale, axis=1)
        return chosen, energy

    chosen, energy = lax.map(per_block, (blocks_in, labels_in))
    return chosen.reshape(PIXELS, ENDMEMBERS), jnp.sum(energy.reshape(N_BLK, N_PIX, BUNDLES), axis=1)
```

```python
import jax
import jax.numpy as jnp
from jax import lax
from jax.experimental import pallas as pl
from jax.experimental.pallas import tpu as pltpu
from jax.sharding import PartitionSpec as P

ITERS = 8
CAP = 16
LANES = 256
ROOT = 0.125
PACK = 4
ALL = ("blk", "pix")
f32, bf16 = jnp.float32, jnp.bfloat16
NT = (((1,), (1,)), ((), ()))


def iota(shape, dim):
    return lax.broadcasted_iota(jnp.int32, shape, dim)


def split(x):
    high = x.astype(bf16)
    return high, (x - high.astype(f32)).astype(bf16)


def dot(a, b):
    return jnp.dot(a, b, preferred_element_type=f32)


def dot_nt(a, b):
    return lax.dot_general(a, b, NT, preferred_element_type=f32)


def prep_kernel(place, bundles, out, wide):
    bands, width = bundles.shape[1:]
    rows = out.shape[1]
    wide[:bands] = bundles[place[0]]
    added = iota((LANES - bands, width), 0) == 0
    wide[bands:] = jnp.where(added, ROOT, 0.0).astype(bf16)
    pick = iota((rows, width), 1) == iota((rows, width), 0) + place[1] * rows
    piece = dot_nt(pick.astype(f32).astype(bf16), wide[...]).astype(bf16)
    for i in range(out.shape[0]):
        out[i] = piece


def slots_kernel(place, labels, pixels, keep, send, code, wide, ranks):
    rows, bands = pixels.shape
    count = rows // (CAP // 2)
    wide[...] = jnp.where(iota(wide.shape, 1) == bands, ROOT, 0.0).astype(bf16)
    wide[:, :bands] = pixels[...]
    label = labels[...]
    chunk = 256
    upper = (iota((chunk, chunk), 0) <= iota((chunk, chunk), 1)).astype(f32).astype(bf16)
    carry = jnp.zeros((count, 1), f32)
    for q in range(rows // chunk):
        part = slice(q * chunk, (q + 1) * chunk)
        named = (iota((count, chunk), 0) == label[:, part]).astype(f32)
        running = dot(named.astype(bf16), upper) + carry
        ranks[:, part] = jnp.sum(named * running, axis=0, keepdims=True) - 1.0
        carry = running[:, chunk - 1 :]
    rank = ranks[...].astype(jnp.int32)
    away = (label & 1) ^ place[0]
    local = ((label >> 1) & 7) * 8 + (label >> 4)
    slot = local * CAP + rank
    kept = jnp.where(away == 0, slot, -1)
    sent = jnp.where(away == 1, slot, -1)
    for key, out in ((kept, keep), (sent, send)):
        for q in range(out.shape[0] // chunk):
            pick = (iota((chunk, rows), 0) + q * chunk == key).astype(f32).astype(bf16)
            out[q * chunk : (q + 1) * chunk] = dot(pick, wide[...]).astype(bf16)
    codes = away * 1024 + (local & 3) * 256 + (local >> 2) * CAP + rank
    code[...] = jnp.broadcast_to(codes.astype(f32), (8, rows)).T


def gathered(bundles, group):
    z = bundles.shape[2]
    tiles = []
    for i in range(PACK * group, PACK * group + PACK):
        tiles += [bundles[i // z, 0, i % z], bundles[i // z, 1, i % z]]
    return jnp.concatenate(tiles, axis=0)


def solve_kernel(place, bundles, mine, theirs, mine_out, theirs_out, energy, high, low, goal, state, steps, sums, parts, scale):
    groups = state.shape[0]
    wide = LANES // PACK
    block = iota((1, LANES), 1) // wide
    same = iota((LANES, LANES), 0) // wide == iota((LANES, LANES), 1) // wide
    for g in range(groups):
        basis = gathered(bundles, g)
        gram = jnp.where(same, dot_nt(basis, basis), 0.0)
        sums[g : g + 1] = jnp.sum(jnp.abs(gram), axis=0, keepdims=True)
        high[g], low[g] = split(gram)
        rows = []
        for i in range(PACK * g, PACK * g + PACK):
            rows += [mine[i * CAP : (i + 1) * CAP], theirs[i * CAP : (i + 1) * CAP]]
        found = dot_nt(jnp.concatenate(rows, axis=0), basis)
        goal[g] = sum(jnp.where(block == i, found[i * 2 * CAP : (i + 1) * 2 * CAP], 0.0) for i in range(PACK))
    total = sums[...]
    largest = jnp.zeros_like(total)
    for i in range(PACK):
        inside = block == i
        largest = jnp.where(inside, jnp.max(jnp.where(inside, total, 0.0), axis=1, keepdims=True), largest)
    steps[...] = 1.0 / largest
    for g in range(groups):
        state[g] = jnp.maximum(steps[g : g + 1] * goal[g], 0.0)

    def sweep(index, carry):
        for g in range(groups):
            a = state[g]
            first, second = split(a)
            both = dot(jnp.concatenate([first, second], axis=0), high[g])
            grad = both[: 2 * CAP] + both[2 * CAP :] + dot(first, low[g])
            state[g] = jnp.maximum(a - steps[g : g + 1] * (grad - goal[g]), 0.0)
        return carry

    lax.fori_loop(1, ITERS, sweep, 0)
    z = bundles.shape[2]
    for g in range(groups):
        a = state[g]
        mine_out[g * CAP : (g + 1) * CAP] = a[:CAP]
        theirs_out[g * CAP : (g + 1) * CAP] = a[CAP:]
        basis = gathered(bundles, g)
        spread = jnp.concatenate([jnp.where(block == i, a, 0.0) for i in range(PACK)], axis=0)
        both = dot(jnp.concatenate(split(spread), axis=0), basis)
        fitted = both[: PACK * 2 * CAP] + both[PACK * 2 * CAP :]
        for i in range(PACK):
            local = PACK * g + i
            rows = slice(local * CAP, (local + 1) * CAP)
            x = jnp.concatenate([mine[rows], theirs[rows]], axis=0).astype(f32)
            misfit = x - fitted[i * 2 * CAP : (i + 1) * 2 * CAP]
            line = jnp.sum(misfit * misfit, axis=0, keepdims=True)
            spot = 2 * (8 * (local % z) + local // z)
            parts[spot : spot + 2] = jnp.broadcast_to(line, (2, LANES))
    bands = LANES - 32
    held = (iota(parts.shape, 1) < bands) & (iota(parts.shape, 0) % 2 == place[0])
    energy[...] = jnp.sum(jnp.where(held, parts[...], 0.0).T, axis=0, keepdims=True) / scale


def return_kernel(code, mine, back, out):
    rows = code.shape[0]
    held = mine.shape[0]
    codes = code[:, :1].astype(jnp.int32)
    place = codes & 255
    pick = iota((rows, 2 * held), 1) == place + (codes >> 10) * held
    pick = pick.astype(f32).astype(bf16)
    table = jnp.concatenate([mine[...], back[...]], axis=0)
    first = table.astype(bf16)
    rest = table - first.astype(f32)
    second, third = split(rest)
    found = dot(pick, first) + dot(pick, second) + dot(pick, third)
    found = jnp.where(iota(found.shape, 1) // 64 == (codes >> 8) & 3, found, 0.0)
    half = found[:, :128] + found[:, 128:]
    out[...] = half[:, :64] + half[:, 64:]


def vmem(shape, dtype):
    return pltpu.VMEM(shape, dtype)


def call(kernel, place, args, outs, scratch):
    spec = pl.BlockSpec(memory_space=pltpu.VMEM)
    smem = [pl.BlockSpec(memory_space=pltpu.SMEM)] if place is not None else []
    head = [place] if place is not None else []
    return pl.pallas_call(
        kernel,
        out_shape=outs,
        in_specs=smem + [spec] * len(args),
        out_specs=jax.tree.map(lambda _: spec, outs),
        scratch_shapes=scratch,
        compiler_params=pltpu.CompilerParams(vmem_limit_bytes=48 << 20),
    )(*head, *args)


def positions(mesh_pix, along_blk):
    spots = []
    for blk in range(along_blk):
        for pix in range(mesh_pix):
            spots.append((blk // 8, blk // 2 % 4, pix // 2, blk % 2, pix % 2))
    return spots


def grouped(spots, key):
    groups = {}
    for index, spot in enumerate(spots):
        groups.setdefault(key(*spot), []).append(index)
    return list(groups.values())


def copies_from(array, groups):
    return lax.all_to_all(array, ALL, 0, 0, tiled=True, axis_index_groups=groups)


def per_device(pixels, bundles, assign):
    rows, bands = pixels.shape
    owned, _, width = bundles.shape
    n_blk, n_pix = lax.axis_size("blk"), lax.axis_size("pix")
    spots = positions(n_pix, n_blk)
    along_z = grouped(spots, lambda z, y, xh, xl, c: (y, xh, xl, c))
    along_yx = grouped(spots, lambda z, y, xh, xl, c: (z, c))
    pix = lax.axis_index("pix")
    place = jnp.stack([pix % 2, pix // 2]).astype(jnp.int32)
    sds = jax.ShapeDtypeStruct
    half = width // 2
    nz, nyx = len(along_z[0]), len(along_yx[0])

    piece = call(prep_kernel, place, [bundles], sds((nz, half, LANES), bf16), [vmem((LANES, width), bf16)])
    column = copies_from(piece, along_z)
    plane = copies_from(jnp.broadcast_to(column[None], (nyx, nz, half, LANES)), along_yx)

    held = (n_blk * owned // 2) * CAP
    keep, send, code = call(
        slots_kernel,
        place,
        [assign.reshape(1, rows), pixels],
        (sds((held, LANES), bf16), sds((held, LANES), bf16), sds((rows, 8), f32)),
        [vmem((rows, LANES), bf16), vmem((1, rows), f32)],
    )
    sibling = [(i, i ^ 1) for i in range(n_pix)]
    theirs = lax.ppermute(send, "pix", sibling)

    groups = held // CAP // PACK
    scale = bands * rows * n_pix / (n_blk * owned)
    mine_out, theirs_out, energy = call(
        lambda *refs: solve_kernel(*refs, scale=scale),
        place,
        [plane.reshape(nyx // 2, 2, nz, half, LANES), keep, theirs],
        (sds((groups * CAP, LANES), f32), sds((groups * CAP, LANES), f32), sds((1, n_blk * owned), f32)),
        [
            vmem((groups, LANES, LANES), bf16),
            vmem((groups, LANES, LANES), bf16),
            vmem((groups, 2 * CAP, LANES), f32),
            vmem((groups, 2 * CAP, LANES), f32),
            vmem((groups, LANES), f32),
            vmem((groups, LANES), f32),
            vmem((n_blk * owned, LANES), f32),
        ],
    )
    back = lax.ppermute(theirs_out, "pix", sibling)
    total = energy
    for flip in range(1, n_pix):
        total = total + lax.ppermute(energy, "pix", [(i, i ^ flip) for i in range(n_pix)])
    chosen = call(return_kernel, None, [code, mine_out, back], sds((rows, width), f32), [])
    return chosen, total


def solution(mesh):
    placed = (P(("blk", "pix"), None), P("blk", None, None), P(("blk", "pix"), None))
    return jax.shard_map(
        per_device,
        mesh=mesh,
        in_specs=placed,
        out_specs=(P(("blk", "pix"), None), P("blk", None)),
        check_vma=False,
    )
```

```python
import jax
import jax.numpy as jnp
from jax import lax
from jax.experimental import pallas as pl
from jax.experimental.pallas import tpu as pltpu
from jax.sharding import PartitionSpec as P

ITERS = 8
CAP = 16
LANES = 256
ROOT = 0.125
PACK = 4
ALL = ("blk", "pix")
f32, bf16 = jnp.float32, jnp.bfloat16


def iota(shape, dim):
    return lax.broadcasted_iota(jnp.int32, shape, dim)


def one_hot(where):
    return where.astype(f32).astype(bf16)


def split(x):
    high = x.astype(bf16)
    return high, (x - high.astype(f32)).astype(bf16)


def dot(a, b):
    return jnp.dot(a, b, preferred_element_type=f32)


def dot_nt(a, b):
    return lax.dot_general(a, b, (((1,), (1,)), ((), ())), preferred_element_type=f32)


def prep_kernel(place, bundles, out):
    width, bands = bundles.shape[1:]
    out[...] = jnp.where(iota(out.shape, 1) == bands, ROOT, 0.0).astype(bf16)
    out[:, :bands] = bundles[place[0]]


def slots_kernel(place, labels, pixels, send, code, wide, ranks):
    bands, rows = pixels.shape
    count = rows // (CAP // 2)
    wide[:bands] = pixels[...]
    wide[bands:] = jnp.where(iota((LANES - bands, rows), 0) == 0, ROOT, 0.0).astype(bf16)
    label = labels[...]
    chunk = 256
    upper = one_hot(iota((chunk, chunk), 0) <= iota((chunk, chunk), 1))
    carry = jnp.zeros((count, 1), f32)
    for q in range(rows // chunk):
        part = slice(q * chunk, (q + 1) * chunk)
        named = (iota((count, chunk), 0) == label[:, part]).astype(f32)
        running = dot(named.astype(bf16), upper) + carry
        ranks[:, part] = jnp.sum(named * running, axis=0, keepdims=True) - 1.0
        carry = running[:, chunk - 1 :]
    rank = ranks[...].astype(jnp.int32)
    handler = (label >> 1 & 1) * 4 + ((label >> 4) + place[2] & 1) * 2 + (label & 1)
    local = (label >> 5) * PACK + (label >> 2 & 3)
    slot = local * CAP + rank
    for d in range(send.shape[0]):
        key = jnp.where(handler == d, slot, -1)
        held = send.shape[1]
        send[d] = dot_nt(one_hot(iota((held, rows), 0) == key), wide[...]).astype(bf16)
    table_row = handler * (held // PACK) + (local >> 2) * CAP + rank
    code[...] = (local & 3) * 1024 + table_row


def solve_kernel(place, bundles, pixels, out, high, low, goal, state, steps, sums, parts, scale):
    groups = state.shape[0]
    sources = pixels.shape[0]
    slots = sources * CAP
    wide = LANES // PACK
    block = iota((1, LANES), 1) // wide
    same = iota((LANES, LANES), 0) // wide == iota((LANES, LANES), 1) // wide

    def basis_of(g):
        return jnp.concatenate([bundles[PACK * g + i] for i in range(PACK)], axis=0)

    def pixels_of(local):
        return jnp.concatenate([pixels[s, local * CAP : (local + 1) * CAP] for s in range(sources)], axis=0)

    for g in range(groups):
        basis = basis_of(g)
        gram = jnp.where(same, dot_nt(basis, basis), 0.0)
        sums[g : g + 1] = jnp.sum(jnp.abs(gram), axis=0, keepdims=True)
        high[g], low[g] = split(gram)
        found = dot_nt(jnp.concatenate([pixels_of(PACK * g + i) for i in range(PACK)], axis=0), basis)
        aim = found[:slots]
        for i in range(1, PACK):
            aim = jnp.where(block == i, found[i * slots : (i + 1) * slots], aim)
        goal[g] = aim
    total = sums[...]
    largest = jnp.zeros_like(total)
    for i in range(PACK):
        inside = block == i
        largest = jnp.where(inside, jnp.max(jnp.where(inside, total, 0.0), axis=1, keepdims=True), largest)
    steps[...] = 1.0 / largest
    for g in range(groups):
        state[g] = jnp.maximum(steps[g : g + 1] * goal[g], 0.0)

    def sweep(index, carry):
        for g in range(groups):
            a = state[g]
            first, second = split(a)
            both = dot(jnp.concatenate([first, second], axis=0), high[g])
            grad = both[:slots] + both[slots:] + dot(first, low[g])
            state[g] = jnp.maximum(a - steps[g : g + 1] * (grad - goal[g]), 0.0)
        return carry

    lax.fori_loop(1, ITERS, sweep, 0)
    parts[...] = jnp.zeros(parts.shape, f32)
    odd = place[2] + place[1] & 1
    for g in range(groups):
        a = state[g]
        for s in range(sources):
            out[s, g * CAP : (g + 1) * CAP] = a[s * CAP : (s + 1) * CAP]
        spread = jnp.concatenate([jnp.where(block == i, a, 0.0) for i in range(PACK)], axis=0)
        both = dot(jnp.concatenate(split(spread), axis=0), basis_of(g))
        fitted = both[: PACK * slots] + both[PACK * slots :]
        for i in range(PACK):
            misfit = pixels_of(PACK * g + i).astype(f32) - fitted[i * slots : (i + 1) * slots]
            square = misfit * misfit
            bundle = 16 * (2 * g + odd) + 4 * i + 2 * place[3] + place[0]
            for half in range(2):
                rows = slice(half * slots // 2, (half + 1) * slots // 2)
                parts[half, pl.ds(bundle, 1), :] = jnp.sum(square[rows], axis=0, keepdims=True)
    bands = LANES - 32
    below = groups * CAP
    for half in range(2):
        lines = parts[half].T
        lines = jnp.where(iota(lines.shape, 0) < bands, lines, 0.0)
        energy = jnp.sum(lines, axis=0, keepdims=True) / scale
        energy = jnp.concatenate([energy, jnp.zeros_like(energy)], axis=1)
        for s in range(half * sources // 2, (half + 1) * sources // 2):
            out[s, below:] = jnp.broadcast_to(energy, (8, LANES))


def return_kernel(code, back, chosen, energy):
    rows = code.shape[1]
    handlers, held, lanes = back.shape
    held -= 8
    wide = lanes // PACK
    codes = code[...]
    pick = one_hot(iota((handlers * held, rows), 0) == codes & 1023)
    table = jnp.concatenate([back[d, :held] for d in range(handlers)], axis=0).T
    first = table.astype(bf16)
    rest = table - first.astype(f32)
    second, third = split(rest)
    found = dot(jnp.concatenate([first, second, third], axis=0), pick)
    found = found[:lanes] + found[lanes : 2 * lanes] + found[2 * lanes :]
    which = codes >> 10
    result = found[:wide]
    for i in range(1, PACK):
        result = jnp.where(which == i, found[i * wide : (i + 1) * wide], result)
    chosen[...] = result
    total = back[0, held : held + 1]
    for d in range(1, handlers):
        total = total + back[d, held : held + 1]
    energy[...] = total[:, : energy.shape[1]]


def vmem(shape, dtype):
    return pltpu.VMEM(shape, dtype)


def call(kernel, place, args, outs, scratch, limit):
    spec = pl.BlockSpec(memory_space=pltpu.VMEM)
    head = [] if place is None else [place]
    return pl.pallas_call(
        kernel,
        out_shape=outs,
        in_specs=[pl.BlockSpec(memory_space=pltpu.SMEM)] * len(head) + [spec] * len(args),
        out_specs=jax.tree.map(lambda _: spec, outs),
        scratch_shapes=scratch,
        compiler_params=pltpu.CompilerParams(vmem_limit_bytes=limit << 20),
    )(*head, *args)


def spots_of(n_blk, n_pix):
    return [(b // 8, b // 2 % 4, b % 2, p // 2, p % 2) for b in range(n_blk) for p in range(n_pix)]


def grouped(spots, key):
    groups = {}
    for index, spot in enumerate(spots):
        groups.setdefault(key(*spot), []).append(index)
    return list(groups.values())


def exchanged(array, groups):
    return lax.all_to_all(array, ALL, 0, 0, tiled=True, axis_index_groups=groups)


def per_device(pixels, bundles, assign):
    rows, bands = pixels.shape
    owned, _, width = bundles.shape
    n_blk, n_pix = lax.axis_size("blk"), lax.axis_size("pix")
    spots = spots_of(n_blk, n_pix)
    column = grouped(spots, lambda z, y, xl, xh, c: (z % 2, xl, xh, c))
    row = grouped(spots, lambda z, y, xl, xh, c: (z, y))
    there = {spot: index for index, spot in enumerate(spots)}
    swap = [(there[s], there[(s[0] ^ s[3],) + s[1:]]) for s in spots]
    blk, pix = lax.axis_index("blk"), lax.axis_index("pix")
    place = jnp.stack([pix & 1, pix >> 1, blk >> 3 & 1, blk & 1]).astype(jnp.int32)
    sds = jax.ShapeDtypeStruct
    n_col, n_row = len(column[0]), len(row[0])
    count = n_blk * owned
    held = n_col * CAP
    groups = n_col // PACK

    basis = call(prep_kernel, place, [bundles.transpose(0, 2, 1)], sds((width, LANES), bf16), [], 4)
    basis = lax.ppermute(basis, ALL, swap)
    send, code = call(
        slots_kernel,
        place,
        [assign.reshape(1, rows), pixels.T],
        (sds((n_row, held, LANES), bf16), sds((1, rows), jnp.int32)),
        [vmem((LANES, rows), bf16), vmem((1, rows), f32)],
        16,
    )
    basis, send = lax.optimization_barrier((basis, send))
    gathered = exchanged(jnp.broadcast_to(basis[None], (n_col, width, LANES)), column)
    received = exchanged(send, row)

    below = groups * CAP
    slots = n_row * CAP
    scale = bands * rows * n_pix / count
    solved = call(
        lambda *refs: solve_kernel(*refs, scale=scale),
        place,
        [gathered, received],
        sds((n_row, below + 8, LANES), f32),
        [
            vmem((groups, LANES, LANES), bf16),
            vmem((groups, LANES, LANES), bf16),
            vmem((groups, slots, LANES), f32),
            vmem((groups, slots, LANES), f32),
            vmem((groups, LANES), f32),
            vmem((groups, LANES), f32),
            vmem((2, count, LANES), f32),
        ],
        16,
    )
    back = exchanged(solved, row)
    chosen, energy = call(
        return_kernel, None, [code, back], (sds((width, rows), f32), sds((1, count), f32)), [], 16
    )
    return chosen.T, energy


def solution(mesh):
    placed = (P(("blk", "pix"), None), P("blk", None, None), P(("blk", "pix"), None))
    return jax.shard_map(
        per_device,
        mesh=mesh,
        in_specs=placed,
        out_specs=(P(("blk", "pix"), None), P("blk", None)),
        check_vma=False,
    )
```

```python
import jax
import jax.numpy as jnp
from jax import lax
from jax.experimental import pallas as pl
from jax.experimental.pallas import tpu as pltpu
from jax.sharding import PartitionSpec as P

ITERS = 8
CAP = 16
LANES = 256
ROOT = 0.125
PACK = 4
ALL = ("blk", "pix")
f32, bf16 = jnp.float32, jnp.bfloat16


def iota(shape, dim):
    return lax.broadcasted_iota(jnp.int32, shape, dim)


def one_hot(where):
    return where.astype(f32).astype(bf16)


def split(x):
    high = x.astype(bf16)
    return high, (x - high.astype(f32)).astype(bf16)


def dot(a, b):
    return jnp.dot(a, b, preferred_element_type=f32)


def dot_nt(a, b):
    return lax.dot_general(a, b, (((1,), (1,)), ((), ())), preferred_element_type=f32)


def prep_kernel(place, bundles, out):
    width, bands = bundles.shape[1:]
    out[...] = jnp.where(iota(out.shape, 1) == bands, ROOT, 0.0).astype(bf16)
    out[:, :bands] = bundles[place[0]]


def slots_kernel(place, labels, pixels, near, away, code, wide, ranks):
    bands, rows = pixels.shape
    count = rows // (CAP // 2)
    wide[:bands] = pixels[...]
    wide[bands:] = jnp.where(iota((LANES - bands, rows), 0) == 0, ROOT, 0.0).astype(bf16)
    label = labels[...]
    chunk = 256
    upper = one_hot(iota((chunk, chunk), 0) <= iota((chunk, chunk), 1))
    carry = jnp.zeros((count, 1), f32)
    for q in range(rows // chunk):
        part = slice(q * chunk, (q + 1) * chunk)
        named = (iota((count, chunk), 0) == label[:, part]).astype(f32)
        running = dot(named.astype(bf16), upper) + carry
        ranks[:, part] = jnp.sum(named * running, axis=0, keepdims=True) - 1.0
        carry = running[:, chunk - 1 :]
    rank = ranks[...].astype(jnp.int32)
    chip = ((label >> 4) + place[2] & 1) * 2 + (label >> 1 & 1)
    handler = (label + place[0] & 1) * 4 + (chip - place[3] & 3)
    local = (label >> 5) * PACK + (label >> 2 & 3)
    slot = local * CAP + rank
    chips, held = near.shape[:2]
    for d in range(2 * chips):
        out = near if d < chips else away
        key = jnp.where(handler == d, slot, -1)
        out[d % chips] = dot_nt(one_hot(iota((held, rows), 0) == key), wide[...]).astype(bf16)
    table_row = handler * (held // PACK) + (local >> 2) * CAP + rank
    code[...] = (local & 3) * 1024 + table_row


def solve_kernel(place, bundles, near, away, moved1, moved2, moved3, *rest, scale):
    outs, (high, low, goal, state, steps, sums, parts) = rest[:4], rest[4:]
    groups = state.shape[0]
    sources = [near.at[0], away.at[0]] + [m.at[i] for m in (moved1, moved2, moved3) for i in range(2)]
    slots = len(sources) * CAP
    wide = LANES // PACK
    block = iota((1, LANES), 1) // wide
    same = iota((LANES, LANES), 0) // wide == iota((LANES, LANES), 1) // wide

    def basis_of(g):
        return jnp.concatenate([bundles[i, g] for i in range(PACK)], axis=0)

    def pixels_of(local):
        return jnp.concatenate([s[local * CAP : (local + 1) * CAP] for s in sources], axis=0)

    for g in range(groups):
        basis = basis_of(g)
        gram = jnp.where(same, dot_nt(basis, basis), 0.0)
        sums[g : g + 1] = jnp.sum(jnp.abs(gram), axis=0, keepdims=True)
        high[g], low[g] = split(gram)
        found = dot_nt(jnp.concatenate([pixels_of(PACK * g + i) for i in range(PACK)], axis=0), basis)
        aim = found[:slots]
        for i in range(1, PACK):
            aim = jnp.where(block == i, found[i * slots : (i + 1) * slots], aim)
        goal[g] = aim
    total = sums[...]
    largest = jnp.zeros_like(total)
    for i in range(PACK):
        inside = block == i
        largest = jnp.where(inside, jnp.max(jnp.where(inside, total, 0.0), axis=1, keepdims=True), largest)
    steps[...] = 1.0 / largest
    for g in range(groups):
        state[g] = jnp.maximum(steps[g : g + 1] * goal[g], 0.0)

    def sweep(index, carry):
        for g in range(groups):
            a = state[g]
            first, second = split(a)
            both = dot(jnp.concatenate([first, second], axis=0), high[g])
            grad = both[:slots] + both[slots:] + dot(first, low[g])
            state[g] = jnp.maximum(a - steps[g : g + 1] * (grad - goal[g]), 0.0)
        return carry

    lax.fori_loop(1, ITERS, sweep, 0)
    parts[...] = jnp.zeros(parts.shape, f32)
    odd = place[2] + place[1] & 1
    for g in range(groups):
        a = state[g]
        for s in range(len(sources)):
            outs[s // 2][s % 2, g * CAP : (g + 1) * CAP] = a[s * CAP : (s + 1) * CAP]
        spread = jnp.concatenate([jnp.where(block == i, a, 0.0) for i in range(PACK)], axis=0)
        both = dot(jnp.concatenate(split(spread), axis=0), basis_of(g))
        fitted = both[: PACK * slots] + both[PACK * slots :]
        for i in range(PACK):
            misfit = pixels_of(PACK * g + i).astype(f32) - fitted[i * slots : (i + 1) * slots]
            square = misfit * misfit
            bundle = 16 * (2 * g + odd) + 4 * i + 2 * (place[3] & 1) + place[0]
            for half in range(2):
                both = square[2 * half * CAP : 2 * (half + 1) * CAP]
                both = both + square[2 * (half + 2) * CAP : 2 * (half + 3) * CAP]
                parts[half, pl.ds(bundle, 1), :] = jnp.sum(both, axis=0, keepdims=True)
    bands = LANES - 32
    below = groups * CAP
    for half in range(2):
        lines = parts[half].T
        lines = jnp.where(iota(lines.shape, 0) < bands, lines, 0.0)
        energy = jnp.sum(lines, axis=0, keepdims=True) / scale
        energy = jnp.concatenate([energy, jnp.zeros_like(energy)], axis=1)
        for r in (half, half + 2):
            for i in range(2):
                outs[r][i, below:] = jnp.broadcast_to(energy, (8, LANES))


def return_kernel(code, back0, back1, back2, back3, others, chosen, energy):
    rows = code.shape[1]
    lanes = others.shape[2]
    held = others.shape[1] - 8
    tables = [b.at[0] for b in (back0, back1, back2, back3)] + [others.at[r] for r in range(others.shape[0])]
    handlers = len(tables)
    wide = lanes // PACK
    codes = code[...]
    pick = one_hot(iota((handlers * held, rows), 0) == codes & 1023)
    table = jnp.concatenate([t[:held] for t in tables], axis=0).T
    first = table.astype(bf16)
    rest = table - first.astype(f32)
    second, third = split(rest)
    found = dot(jnp.concatenate([first, second, third], axis=0), pick)
    found = found[:lanes] + found[lanes : 2 * lanes] + found[2 * lanes :]
    which = codes >> 10
    result = found[:wide]
    for i in range(1, PACK):
        result = jnp.where(which == i, found[i * wide : (i + 1) * wide], result)
    chosen[...] = result
    total = tables[0][held : held + 1]
    for t in tables[1:]:
        total = total + t[held : held + 1]
    energy[...] = total[:, : energy.shape[1]]


def vmem(shape, dtype):
    return pltpu.VMEM(shape, dtype)


def call(kernel, place, args, outs, scratch, limit):
    spec = pl.BlockSpec(memory_space=pltpu.VMEM)
    head = [] if place is None else [place]
    return pl.pallas_call(
        kernel,
        out_shape=outs,
        in_specs=[pl.BlockSpec(memory_space=pltpu.SMEM)] * len(head) + [spec] * len(args),
        out_specs=jax.tree.map(lambda _: spec, outs),
        scratch_shapes=scratch,
        compiler_params=pltpu.CompilerParams(vmem_limit_bytes=limit << 20),
    )(*head, *args)


def spots_of(n_blk, n_pix):
    return [(b // 8, b // 2 % 4, b % 2, p // 2, p % 2) for b in range(n_blk) for p in range(n_pix)]


def grouped(spots, key):
    groups = {}
    for index, spot in enumerate(spots):
        groups.setdefault(key(*spot), []).append(index)
    return list(groups.values())


def exchanged(array, groups):
    return lax.all_to_all(array, ALL, 0, 0, tiled=True, axis_index_groups=groups)


def per_device(pixels, bundles, assign):
    rows, bands = pixels.shape
    owned, _, width = bundles.shape
    n_blk, n_pix = lax.axis_size("blk"), lax.axis_size("pix")
    spots = spots_of(n_blk, n_pix)
    along_z = grouped(spots, lambda z, y, xl, xh, c: (y, xl, xh, c))
    along_y = grouped(spots, lambda z, y, xl, xh, c: (z, xl, xh, c))
    there = {spot: index for index, spot in enumerate(spots)}

    def shifted(array, r):
        pairs = []
        for z, y, xl, xh, c in spots:
            x = (2 * xh + xl + r) % 4
            pairs.append((there[z, y, xl, xh, c], there[z, y, x % 2, x // 2, c]))
        return lax.ppermute(array, ALL, pairs)

    def to_sibling(array):
        return lax.ppermute(array, ALL, [(i, i ^ 1) for i in range(len(spots))])

    blk, pix = lax.axis_index("blk"), lax.axis_index("pix")
    z, x_hi = blk >> 3, pix >> 1
    place = jnp.stack([pix & 1, x_hi, z & 1, 2 * x_hi + (blk & 1)]).astype(jnp.int32)
    sds = jax.ShapeDtypeStruct
    n_z, n_y = len(along_z[0]), len(along_y[0])
    chips = 4
    count = n_blk * owned
    groups = n_z // 2
    held = groups * n_y * CAP

    basis = call(prep_kernel, place, [bundles.transpose(0, 2, 1)], sds((width, LANES), bf16), [], 4)
    levels = exchanged(jnp.broadcast_to(basis[None], (n_z, width, LANES)), along_z)
    near, away, code = call(
        slots_kernel,
        place,
        [assign.reshape(1, rows), pixels.T],
        (sds((chips, held, LANES), bf16), sds((chips, held, LANES), bf16), sds((1, rows), jnp.int32)),
        [vmem((LANES, rows), bf16), vmem((1, rows), f32)],
        16,
    )
    theirs = to_sibling(away)
    moved = [shifted(jnp.stack([near[r], theirs[r]]), r) for r in range(1, chips)]
    half = lax.dynamic_index_in_dim(levels.reshape(groups, 2, width, LANES), (z + x_hi) & 1, 1, keepdims=False)
    plane = exchanged(jnp.broadcast_to(half[None], (n_y, groups, width, LANES)), along_y)

    below = groups * CAP
    slots = 2 * chips * CAP
    scale = bands * rows * n_pix / count
    solved = call(
        lambda *refs: solve_kernel(*refs, scale=scale),
        place,
        [plane, near, theirs, *moved],
        (sds((2, below + 8, LANES), f32),) * chips,
        [
            vmem((groups, LANES, LANES), bf16),
            vmem((groups, LANES, LANES), bf16),
            vmem((groups, slots, LANES), f32),
            vmem((groups, slots, LANES), f32),
            vmem((groups, LANES), f32),
            vmem((groups, LANES), f32),
            vmem((2, count, LANES), f32),
        ],
        16,
    )
    back = [solved[0]] + [shifted(solved[r], -r) for r in range(1, chips)]
    others = to_sibling(jnp.stack([b[1] for b in back]))
    outs = (sds((width, rows), f32), sds((1, count), f32))
    chosen, energy = call(return_kernel, None, [code, *back, others], outs, [], 16)
    return chosen.T, energy


def solution(mesh):
    placed = (P(("blk", "pix"), None), P("blk", None, None), P(("blk", "pix"), None))
    return jax.shard_map(
        per_device,
        mesh=mesh,
        in_specs=placed,
        out_specs=(P(("blk", "pix"), None), P("blk", None)),
        check_vma=False,
    )
```

```python
import jax
import jax.numpy as jnp
from jax import lax
from jax.experimental import pallas as pl
from jax.experimental.pallas import tpu as pltpu
from jax.sharding import PartitionSpec as P

ITERS = 8
CAP = 16
LANES = 256
ROOT = 0.125
PACK = 4
ALL = ("blk", "pix")
f32, bf16 = jnp.float32, jnp.bfloat16


def iota(shape, dim):
    return lax.broadcasted_iota(jnp.int32, shape, dim)


def one_hot(where):
    return where.astype(f32).astype(bf16)


def split(x):
    high = x.astype(bf16)
    return high, (x - high.astype(f32)).astype(bf16)


def dot(a, b):
    return jnp.dot(a, b, preferred_element_type=f32)


def dot_nt(a, b):
    return lax.dot_general(a, b, (((1,), (1,)), ((), ())), preferred_element_type=f32)


def prep_kernel(place, bundles, out):
    width, bands = bundles.shape[1:]
    out[...] = jnp.where(iota(out.shape, 1) == bands, ROOT, 0.0).astype(bf16)
    out[:, :bands] = bundles[place[0]]


def slots_kernel(place, labels, pixels, *rest):
    outs, (code, wide, ranks) = rest[:-3], rest[-3:]
    bands, rows = pixels.shape
    count = rows // (CAP // 2)
    wide[:bands] = pixels[...]
    wide[bands:] = jnp.where(iota((LANES - bands, rows), 0) == 0, ROOT, 0.0).astype(bf16)
    label = labels[...]
    chunk = 256
    upper = one_hot(iota((chunk, chunk), 0) <= iota((chunk, chunk), 1))
    carry = jnp.zeros((count, 1), f32)
    for q in range(rows // chunk):
        part = slice(q * chunk, (q + 1) * chunk)
        named = (iota((count, chunk), 0) == label[:, part]).astype(f32)
        running = dot(named.astype(bf16), upper) + carry
        ranks[:, part] = jnp.sum(named * running, axis=0, keepdims=True) - 1.0
        carry = running[:, chunk - 1 :]
    rank = ranks[...].astype(jnp.int32)
    chip = ((label >> 4) + place[2] & 1) * 2 + (label >> 1 & 1)
    handler = (chip - place[3] & 3) * 2 + (label + place[0] & 1)
    local = (label >> 5) * PACK + (label >> 2 & 3)
    slot = local * CAP + rank
    held = outs[0].shape[0]
    for d in range(len(outs)):
        key = jnp.where(handler == d, slot, -1)
        outs[d][...] = dot_nt(one_hot(iota((held, rows), 0) == key), wide[...]).astype(bf16)
    table_row = handler * (held // PACK) + (local >> 2) * CAP + rank
    code[...] = (local & 3) * 1024 + table_row


def pick_kernel(place, levels, *rest):
    out = rest[-1]
    odd = place[2] + place[1] & 1
    for g in range(out.shape[1]):
        level = levels[2 * g + odd]
        for y in range(out.shape[0]):
            out[y, g] = level


def solve_kernel(place, bundles, *rest, scale):
    sources, outs = rest[:-9], rest[-9:-7]
    high, low, goal, state, steps, sums, parts = rest[-7:]
    groups = state.shape[0]
    slots = len(sources) * CAP
    wide = LANES // PACK
    block = iota((1, LANES), 1) // wide
    same = iota((LANES, LANES), 0) // wide == iota((LANES, LANES), 1) // wide

    def basis_of(g):
        return jnp.concatenate([bundles[i, g] for i in range(PACK)], axis=0)

    def pixels_of(local):
        return jnp.concatenate([s[local * CAP : (local + 1) * CAP] for s in sources], axis=0)

    for g in range(groups):
        basis = basis_of(g)
        gram = jnp.where(same, dot_nt(basis, basis), 0.0)
        sums[g : g + 1] = jnp.sum(jnp.abs(gram), axis=0, keepdims=True)
        high[g], low[g] = split(gram)
        found = dot_nt(jnp.concatenate([pixels_of(PACK * g + i) for i in range(PACK)], axis=0), basis)
        aim = found[:slots]
        for i in range(1, PACK):
            aim = jnp.where(block == i, found[i * slots : (i + 1) * slots], aim)
        goal[g] = aim
    total = sums[...]
    largest = jnp.zeros_like(total)
    for i in range(PACK):
        inside = block == i
        largest = jnp.where(inside, jnp.max(jnp.where(inside, total, 0.0), axis=1, keepdims=True), largest)
    steps[...] = 1.0 / largest
    for g in range(groups):
        state[g] = jnp.maximum(steps[g : g + 1] * goal[g], 0.0)

    def sweep(index, carry):
        for g in range(groups):
            a = state[g]
            first, second = split(a)
            both = dot(jnp.concatenate([first, second], axis=0), high[g])
            grad = both[:slots] + both[slots:] + dot(first, low[g])
            state[g] = jnp.maximum(a - steps[g : g + 1] * (grad - goal[g]), 0.0)
        return carry

    lax.fori_loop(1, ITERS, sweep, 0)
    parts[...] = jnp.zeros(parts.shape, f32)
    odd = place[2] + place[1] & 1
    for g in range(groups):
        a = state[g]
        for s in range(len(sources)):
            outs[s % 2][s // 2, g * CAP : (g + 1) * CAP] = a[s * CAP : (s + 1) * CAP]
        spread = jnp.concatenate([jnp.where(block == i, a, 0.0) for i in range(PACK)], axis=0)
        both = dot(jnp.concatenate(split(spread), axis=0), basis_of(g))
        fitted = both[: PACK * slots] + both[PACK * slots :]
        for i in range(PACK):
            misfit = pixels_of(PACK * g + i).astype(f32) - fitted[i * slots : (i + 1) * slots]
            square = misfit * misfit
            bundle = 16 * (2 * g + odd) + 4 * i + 2 * (place[3] & 1) + place[0]
            for half in range(2):
                both = square[2 * half * CAP : 2 * (half + 1) * CAP]
                both = both + square[2 * (half + 2) * CAP : 2 * (half + 3) * CAP]
                parts[half, pl.ds(bundle, 1), :] = jnp.sum(both, axis=0, keepdims=True)
    bands = LANES - 32
    below = groups * CAP
    for half in range(2):
        lines = parts[half].T
        lines = jnp.where(iota(lines.shape, 0) < bands, lines, 0.0)
        energy = jnp.sum(lines, axis=0, keepdims=True) / scale
        energy = jnp.concatenate([energy, jnp.zeros_like(energy)], axis=1)
        for r in (half, half + 2):
            for i in range(2):
                outs[i][r, below:] = jnp.broadcast_to(energy, (8, LANES))


def return_kernel(code, mine, theirs, back1, back2, back3, chosen, energy):
    rows = code.shape[1]
    held, lanes = mine.shape[1] - 8, mine.shape[2]
    backs = (back1, back2, back3)
    tables = [mine.at[0], theirs.at[0]] + [b.at[i] for b in backs for i in range(2)]
    handlers = len(tables)
    wide = lanes // PACK
    codes = code[...]
    pick = one_hot(iota((handlers * held, rows), 0) == codes & 1023)
    table = jnp.concatenate([t[:held] for t in tables], axis=0).T
    first = table.astype(bf16)
    rest = table - first.astype(f32)
    second, third = split(rest)
    found = dot(jnp.concatenate([first, second, third], axis=0), pick)
    found = found[:lanes] + found[lanes : 2 * lanes] + found[2 * lanes :]
    which = codes >> 10
    result = found[:wide]
    for i in range(1, PACK):
        result = jnp.where(which == i, found[i * wide : (i + 1) * wide], result)
    chosen[...] = result
    total = tables[0][held : held + 1]
    for t in tables[1:]:
        total = total + t[held : held + 1]
    energy[...] = total[:, : energy.shape[1]]


def vmem(shape, dtype):
    return pltpu.VMEM(shape, dtype)


def call(kernel, place, args, outs, scratch, limit, after=()):
    spec = pl.BlockSpec(memory_space=pltpu.VMEM)
    head = [] if place is None else [place]
    return pl.pallas_call(
        kernel,
        out_shape=outs,
        in_specs=[pl.BlockSpec(memory_space=pltpu.SMEM)] * len(head) + [spec] * len(args) + [pl.BlockSpec(memory_space=pl.ANY)] * len(after),
        out_specs=jax.tree.map(lambda _: spec, outs),
        scratch_shapes=scratch,
        compiler_params=pltpu.CompilerParams(vmem_limit_bytes=limit << 20),
    )(*head, *args, *after)


def spots_of(n_blk, n_pix):
    return [(b // 8, b // 2 % 4, b % 2, p // 2, p % 2) for b in range(n_blk) for p in range(n_pix)]


def grouped(spots, key):
    groups = {}
    for index, spot in enumerate(spots):
        groups.setdefault(key(*spot), []).append(index)
    return list(groups.values())


def exchanged(array, groups):
    return lax.all_to_all(array, ALL, 0, 0, tiled=True, axis_index_groups=groups)


def per_device(pixels, bundles, assign):
    rows, bands = pixels.shape
    owned, _, width = bundles.shape
    n_blk, n_pix = lax.axis_size("blk"), lax.axis_size("pix")
    spots = spots_of(n_blk, n_pix)
    along_z = grouped(spots, lambda z, y, xl, xh, c: (y, xl, xh, c))
    along_y = grouped(spots, lambda z, y, xl, xh, c: (z, xl, xh, c))
    there = {spot: index for index, spot in enumerate(spots)}

    def moved(array, r, other):
        pairs = []
        for z, y, xl, xh, c in spots:
            x = (2 * xh + xl + r) % 4
            pairs.append((there[z, y, xl, xh, c], there[z, y, x % 2, x // 2, c ^ other]))
        return lax.ppermute(array, ALL, pairs) if r or other else array

    blk, pix = lax.axis_index("blk"), lax.axis_index("pix")
    z, x_hi = blk >> 3, pix >> 1
    place = jnp.stack([pix & 1, x_hi, z & 1, 2 * x_hi + (blk & 1)]).astype(jnp.int32)
    sds = jax.ShapeDtypeStruct
    n_z, n_y = len(along_z[0]), len(along_y[0])
    chips = 4
    count = n_blk * owned
    groups = n_z // 2
    held = groups * n_y * CAP

    basis = call(prep_kernel, place, [bundles.transpose(0, 2, 1)], sds((width, LANES), bf16), [], 4)
    levels = exchanged(jnp.broadcast_to(basis[None], (n_z, width, LANES)), along_z)
    *sends, code = call(
        slots_kernel,
        place,
        [assign.reshape(1, rows), pixels.T],
        (sds((held, LANES), bf16),) * (2 * chips) + (sds((1, rows), jnp.int32),),
        [vmem((LANES, rows), bf16), vmem((1, rows), f32)],
        16,
    )
    received = [moved(send, d // 2, d % 2) for d, send in enumerate(sends)]
    half = call(pick_kernel, place, [levels], sds((n_y, groups, width, LANES), bf16), [], 4, received[2::2])
    plane = exchanged(half, along_y)

    below = groups * CAP
    slots = 2 * chips * CAP
    scale = bands * rows * n_pix / count
    solved = call(
        lambda *refs: solve_kernel(*refs, scale=scale),
        place,
        [plane, *received],
        (sds((chips, below + 8, LANES), f32),) * 2,
        [
            vmem((groups, LANES, LANES), bf16),
            vmem((groups, LANES, LANES), bf16),
            vmem((groups, slots, LANES), f32),
            vmem((groups, slots, LANES), f32),
            vmem((groups, LANES), f32),
            vmem((groups, LANES), f32),
            vmem((2, count, LANES), f32),
        ],
        16,
    )
    mine, others = solved[0], moved(solved[1], 0, 1)
    back = [moved(jnp.stack([mine[r], others[r]]), -r, 0) for r in range(1, chips)]
    outs = (sds((width, rows), f32), sds((1, count), f32))
    chosen, energy = call(return_kernel, None, [code, mine, others, *back], outs, [], 16)
    return chosen.T, energy


def solution(mesh):
    placed = (P(("blk", "pix"), None), P("blk", None, None), P(("blk", "pix"), None))
    return jax.shard_map(
        per_device,
        mesh=mesh,
        in_specs=placed,
        out_specs=(P(("blk", "pix"), None), P("blk", None)),
        check_vma=False,
    )
```

```python
import jax
import jax.numpy as jnp
from jax import lax
from jax.experimental import pallas as pl
from jax.experimental.pallas import tpu as pltpu
from jax.sharding import PartitionSpec as P

ITERS = 8
CAP = 16
LANES = 256
ROOT = 0.125
PACK = 4
ALL = ("blk", "pix")
f32, bf16 = jnp.float32, jnp.bfloat16


def iota(shape, dim):
    return lax.broadcasted_iota(jnp.int32, shape, dim)


def one_hot(where):
    return where.astype(f32).astype(bf16)


def split(x):
    high = x.astype(bf16)
    return high, (x - high.astype(f32)).astype(bf16)


def dot(a, b):
    return jnp.dot(a, b, preferred_element_type=f32)


def dot_nt(a, b):
    return lax.dot_general(a, b, (((1,), (1,)), ((), ())), preferred_element_type=f32)


def prep_kernel(place, bundles, out):
    width, bands = bundles.shape[1:]
    out[...] = jnp.where(iota(out.shape, 1) == bands, ROOT, 0.0).astype(bf16)
    out[:, :bands] = bundles[place[0]]


def slots_kernel(place, labels, pixels, *rest):
    outs, (code, wide, ranks) = rest[:-3], rest[-3:]
    bands, rows = pixels.shape
    count = rows // (CAP // 2)
    wide[:bands] = pixels[...]
    wide[bands:] = jnp.where(iota((LANES - bands, rows), 0) == 0, ROOT, 0.0).astype(bf16)
    label = labels[...]
    chunk = 256
    upper = one_hot(iota((chunk, chunk), 0) <= iota((chunk, chunk), 1))
    carry = jnp.zeros((count, 1), f32)
    for q in range(rows // chunk):
        part = slice(q * chunk, (q + 1) * chunk)
        named = (iota((count, chunk), 0) == label[:, part]).astype(f32)
        running = dot(named.astype(bf16), upper) + carry
        ranks[:, part] = jnp.sum(named * running, axis=0, keepdims=True) - 1.0
        carry = running[:, chunk - 1 :]
    rank = ranks[...].astype(jnp.int32)
    other = (label >> 6) ^ place[2]
    chip = other * 2 + (label >> 1 & 1)
    handler = (chip - place[3] & 3) * 2 + (label + place[0] & 1)
    local = ((label >> 4 & 3) ^ other * 3) * PACK + (label >> 2 & 3)
    slot = local * CAP + rank
    held = outs[0].shape[0]
    for d in range(len(outs)):
        key = jnp.where(handler == d, slot, -1)
        outs[d][...] = dot_nt(one_hot(iota((held, rows), 0) == key), wide[...]).astype(bf16)
    table_row = handler * (held // PACK) + (local >> 2) * CAP + rank
    code[...] = (local & 3) * 1024 + table_row


def repeat_kernel(basis, *rest):
    out = rest[-1]
    for i in range(out.shape[0]):
        out[i] = basis[...]


def solve_kernel(place, bundles, *rest, scale):
    sources, outs = rest[:-9], rest[-9:-7]
    high, low, goal, state, steps, sums, parts = rest[-7:]
    groups = state.shape[0]
    slots = len(sources) * CAP
    wide = LANES // PACK
    block = iota((1, LANES), 1) // wide
    same = iota((LANES, LANES), 0) // wide == iota((LANES, LANES), 1) // wide

    def basis_of(g):
        return jnp.concatenate([bundles[PACK * g + i] for i in range(PACK)], axis=0)

    def pixels_of(local):
        return jnp.concatenate([s[local * CAP : (local + 1) * CAP] for s in sources], axis=0)

    for g in range(groups):
        basis = basis_of(g)
        gram = jnp.where(same, dot_nt(basis, basis), 0.0)
        sums[g : g + 1] = jnp.sum(jnp.abs(gram), axis=0, keepdims=True)
        high[g], low[g] = split(gram)
        found = dot_nt(jnp.concatenate([pixels_of(PACK * g + i) for i in range(PACK)], axis=0), basis)
        aim = found[:slots]
        for i in range(1, PACK):
            aim = jnp.where(block == i, found[i * slots : (i + 1) * slots], aim)
        goal[g] = aim
    total = sums[...]
    largest = jnp.zeros_like(total)
    for i in range(PACK):
        inside = block == i
        largest = jnp.where(inside, jnp.max(jnp.where(inside, total, 0.0), axis=1, keepdims=True), largest)
    steps[...] = 1.0 / largest
    for g in range(groups):
        state[g] = jnp.maximum(steps[g : g + 1] * goal[g], 0.0)

    def sweep(index, carry):
        for g in range(groups):
            a = state[g]
            first, second = split(a)
            both = dot(jnp.concatenate([first, second], axis=0), high[g])
            grad = both[:slots] + both[slots:] + dot(first, low[g])
            state[g] = jnp.maximum(a - steps[g : g + 1] * (grad - goal[g]), 0.0)
        return carry

    lax.fori_loop(1, ITERS, sweep, 0)
    parts[...] = jnp.zeros(parts.shape, f32)
    for g in range(groups):
        a = state[g]
        for s in range(len(sources)):
            outs[s % 2][s // 2, g * CAP : (g + 1) * CAP] = a[s * CAP : (s + 1) * CAP]
        spread = jnp.concatenate([jnp.where(block == i, a, 0.0) for i in range(PACK)], axis=0)
        both = dot(jnp.concatenate(split(spread), axis=0), basis_of(g))
        fitted = both[: PACK * slots] + both[PACK * slots :]
        for i in range(PACK):
            misfit = pixels_of(PACK * g + i).astype(f32) - fitted[i * slots : (i + 1) * slots]
            square = misfit * misfit
            bundle = 16 * (4 * place[2] + g ^ 7 * place[1]) + 4 * i + 2 * (place[3] & 1) + place[0]
            for half in range(2):
                both = square[2 * half * CAP : 2 * (half + 1) * CAP]
                both = both + square[2 * (half + 2) * CAP : 2 * (half + 3) * CAP]
                parts[half, pl.ds(bundle, 1), :] = jnp.sum(both, axis=0, keepdims=True)
    bands = LANES - 32
    below = groups * CAP
    for half in range(2):
        lines = parts[half].T
        lines = jnp.where(iota(lines.shape, 0) < bands, lines, 0.0)
        energy = jnp.sum(lines, axis=0, keepdims=True) / scale
        energy = jnp.concatenate([energy, jnp.zeros_like(energy)], axis=1)
        for r in (half, half + 2):
            for i in range(2):
                outs[i][r, below:] = jnp.broadcast_to(energy, (8, LANES))


def return_kernel(code, mine, theirs, back1, back2, back3, chosen, energy):
    rows = code.shape[1]
    held, lanes = mine.shape[1] - 8, mine.shape[2]
    backs = (back1, back2, back3)
    tables = [mine.at[0], theirs.at[0]] + [b.at[i] for b in backs for i in range(2)]
    handlers = len(tables)
    wide = lanes // PACK
    codes = code[...]
    pick = one_hot(iota((handlers * held, rows), 0) == codes & 1023)
    table = jnp.concatenate([t[:held] for t in tables], axis=0).T
    first = table.astype(bf16)
    rest = table - first.astype(f32)
    second, third = split(rest)
    found = dot(jnp.concatenate([first, second, third], axis=0), pick)
    found = found[:lanes] + found[lanes : 2 * lanes] + found[2 * lanes :]
    which = codes >> 10
    result = found[:wide]
    for i in range(1, PACK):
        result = jnp.where(which == i, found[i * wide : (i + 1) * wide], result)
    chosen[...] = result
    total = tables[0][held : held + 1]
    for t in tables[1:]:
        total = total + t[held : held + 1]
    energy[...] = total[:, : energy.shape[1]]


def vmem(shape, dtype):
    return pltpu.VMEM(shape, dtype)


def call(kernel, place, args, outs, scratch, limit, after=()):
    spec = pl.BlockSpec(memory_space=pltpu.VMEM)
    head = [] if place is None else [place]
    return pl.pallas_call(
        kernel,
        out_shape=outs,
        in_specs=[pl.BlockSpec(memory_space=pltpu.SMEM)] * len(head) + [spec] * len(args) + [pl.BlockSpec(memory_space=pl.ANY)] * len(after),
        out_specs=jax.tree.map(lambda _: spec, outs),
        scratch_shapes=scratch,
        compiler_params=pltpu.CompilerParams(vmem_limit_bytes=limit << 20),
    )(*head, *args, *after)


def spots_of(n_blk, n_pix):
    return [(b // 8, b // 2 % 4, b % 2, p // 2, p % 2) for b in range(n_blk) for p in range(n_pix)]


def grouped(spots, key):
    groups = {}
    for index, spot in enumerate(spots):
        groups.setdefault(key(*spot), []).append(index)
    return list(groups.values())


def exchanged(array, groups):
    return lax.all_to_all(array, ALL, 0, 0, tiled=True, axis_index_groups=groups)


def per_device(pixels, bundles, assign):
    rows, bands = pixels.shape
    owned, _, width = bundles.shape
    n_blk, n_pix = lax.axis_size("blk"), lax.axis_size("pix")
    spots = spots_of(n_blk, n_pix)
    column = grouped(spots, lambda z, y, xl, xh, c: (z // 4, xl, xh, c))
    there = {spot: index for index, spot in enumerate(spots)}
    swap = [(there[s], there[(s[0] ^ 7 * s[3],) + s[1:]]) for s in spots]

    def moved(array, r, other):
        pairs = []
        for z, y, xl, xh, c in spots:
            x = (2 * xh + xl + r) % 4
            pairs.append((there[z, y, xl, xh, c], there[z, y, x % 2, x // 2, c ^ other]))
        return lax.ppermute(array, ALL, pairs) if r or other else array

    blk, pix = lax.axis_index("blk"), lax.axis_index("pix")
    z, x_hi = blk >> 3, pix >> 1
    place = jnp.stack([pix & 1, x_hi, z >> 2, 2 * x_hi + (blk & 1)]).astype(jnp.int32)
    sds = jax.ShapeDtypeStruct
    n_col, chips = len(column[0]), 4
    count = n_blk * owned
    groups = n_col // PACK
    held = n_col * CAP

    basis = call(prep_kernel, place, [bundles.transpose(0, 2, 1)], sds((width, LANES), bf16), [], 4)
    basis = lax.ppermute(basis, ALL, swap)
    *sends, code = call(
        slots_kernel,
        place,
        [assign.reshape(1, rows), pixels.T],
        (sds((held, LANES), bf16),) * (2 * chips) + (sds((1, rows), jnp.int32),),
        [vmem((LANES, rows), bf16), vmem((1, rows), f32)],
        16,
    )
    basis = call(repeat_kernel, None, [basis], sds((n_col, width, LANES), bf16), [], 4, [sends[0]])
    gathered = exchanged(basis, column)
    received = [moved(send, d // 2, d % 2) for d, send in enumerate(sends)]

    below = groups * CAP
    slots = 2 * chips * CAP
    scale = bands * rows * n_pix / count
    solved = call(
        lambda *refs: solve_kernel(*refs, scale=scale),
        place,
        [gathered, *received],
        (sds((chips, below + 8, LANES), f32),) * 2,
        [
            vmem((groups, LANES, LANES), bf16),
            vmem((groups, LANES, LANES), bf16),
            vmem((groups, slots, LANES), f32),
            vmem((groups, slots, LANES), f32),
            vmem((groups, LANES), f32),
            vmem((groups, LANES), f32),
            vmem((2, count, LANES), f32),
        ],
        16,
    )
    mine, others = solved[0], moved(solved[1], 0, 1)
    back = [moved(jnp.stack([mine[r], others[r]]), -r, 0) for r in range(1, chips)]
    outs = (sds((width, rows), f32), sds((1, count), f32))
    chosen, energy = call(return_kernel, None, [code, mine, others, *back], outs, [], 16)
    return chosen.T, energy


def solution(mesh):
    placed = (P(("blk", "pix"), None), P("blk", None, None), P(("blk", "pix"), None))
    return jax.shard_map(
        per_device,
        mesh=mesh,
        in_specs=placed,
        out_specs=(P(("blk", "pix"), None), P("blk", None)),
        check_vma=False,
    )
```

```python
import jax
import jax.numpy as jnp
from jax import lax
from jax.experimental import pallas as pl
from jax.experimental.pallas import tpu as pltpu
from jax.sharding import PartitionSpec as P

ITERS = 8
CAP = 16
LANES = 256
ROOT = 0.125
PACK = 4
ALL = ("blk", "pix")
f32, bf16 = jnp.float32, jnp.bfloat16


def iota(shape, dim):
    return lax.broadcasted_iota(jnp.int32, shape, dim)


def one_hot(where):
    return where.astype(f32).astype(bf16)


def split(x):
    high = x.astype(bf16)
    return high, (x - high.astype(f32)).astype(bf16)


def dot(a, b):
    return jnp.dot(a, b, preferred_element_type=f32)


def dot_nt(a, b):
    return lax.dot_general(a, b, (((1,), (1,)), ((), ())), preferred_element_type=f32)


def spread_kernel(place, bundles, *rest):
    out, wide = rest[-2:]
    bands = bundles.shape[2]
    wide[...] = jnp.where(iota(wide.shape, 1) == bands, ROOT, 0.0).astype(bf16)
    wide[:, :bands] = bundles[place[0]]
    for i in range(out.shape[0]):
        out[i] = wide[...]


def slots_kernel(place, labels, pixels, *rest):
    outs, (code, wide, ranks) = rest[:-3], rest[-3:]
    bands, rows = pixels.shape
    count = rows // (CAP // 2)
    wide[:bands] = pixels[...]
    wide[bands:] = jnp.where(iota((LANES - bands, rows), 0) == 0, ROOT, 0.0).astype(bf16)
    label = labels[...]
    chunk = 256
    upper = one_hot(iota((chunk, chunk), 0) <= iota((chunk, chunk), 1))
    carry = jnp.zeros((count, 1), f32)
    for q in range(rows // chunk):
        part = slice(q * chunk, (q + 1) * chunk)
        named = (iota((count, chunk), 0) == label[:, part]).astype(f32)
        running = dot(named.astype(bf16), upper) + carry
        ranks[:, part] = jnp.sum(named * running, axis=0, keepdims=True) - 1.0
        carry = running[:, chunk - 1 :]
    rank = ranks[...].astype(jnp.int32)
    other = (label >> 6) ^ place[2]
    chip = other * 2 + (label >> 1 & 1)
    handler = (chip - place[3] & 3) * 2 + (label + place[0] & 1)
    local = ((label >> 4 & 3) ^ other * 3) * PACK + (label >> 2 & 3)
    slot = local * CAP + rank
    held = outs[0].shape[1]
    for d in range(2 * len(outs)):
        key = jnp.where(handler == d, slot, -1)
        outs[d // 2][d % 2] = dot_nt(one_hot(iota((held, rows), 0) == key), wide[...]).astype(bf16)
    table_row = handler * (held // PACK) + (local >> 2) * CAP + rank
    code[...] = (local & 3) * 1024 + table_row


def stack_kernel(*refs):
    for r, m in enumerate(refs[:-1]):
        refs[-1][r] = m[1]


def solve_kernel(place, bundles, theirs, *rest, scale):
    sources = [s for r, m in enumerate(rest[:-9]) for s in (m.at[0], theirs.at[r])]
    outs = rest[-9:-7]
    high, low, goal, state, steps, sums, parts = rest[-7:]
    groups = state.shape[0]
    slots = len(sources) * CAP
    wide = LANES // PACK
    block = iota((1, LANES), 1) // wide
    same = iota((LANES, LANES), 0) // wide == iota((LANES, LANES), 1) // wide

    def basis_of(g):
        return jnp.concatenate([bundles[PACK * g + i] for i in range(PACK)], axis=0)

    def pixels_of(local):
        return jnp.concatenate([s[local * CAP : (local + 1) * CAP] for s in sources], axis=0)

    for g in range(groups):
        basis = basis_of(g)
        gram = jnp.where(same, dot_nt(basis, basis), 0.0)
        sums[g : g + 1] = jnp.sum(jnp.abs(gram), axis=0, keepdims=True)
        high[g], low[g] = split(gram)
        found = dot_nt(jnp.concatenate([pixels_of(PACK * g + i) for i in range(PACK)], axis=0), basis)
        aim = found[:slots]
        for i in range(1, PACK):
            aim = jnp.where(block == i, found[i * slots : (i + 1) * slots], aim)
        goal[g] = aim
    total = sums[...]
    largest = jnp.zeros_like(total)
    for i in range(PACK):
        inside = block == i
        largest = jnp.where(inside, jnp.max(jnp.where(inside, total, 0.0), axis=1, keepdims=True), largest)
    steps[...] = 1.0 / largest
    for g in range(groups):
        state[g] = jnp.maximum(steps[g : g + 1] * goal[g], 0.0)

    def sweep(index, carry):
        for g in range(groups):
            a = state[g]
            first, second = split(a)
            both = dot(jnp.concatenate([first, second], axis=0), high[g])
            grad = both[:slots] + both[slots:] + dot(first, low[g])
            state[g] = jnp.maximum(a - steps[g : g + 1] * (grad - goal[g]), 0.0)
        return carry

    lax.fori_loop(1, ITERS, sweep, 0)
    parts[...] = jnp.zeros(parts.shape, f32)
    for g in range(groups):
        a = state[g]
        for s in range(len(sources)):
            outs[s % 2][s // 2, g * CAP : (g + 1) * CAP] = a[s * CAP : (s + 1) * CAP]
        spread = jnp.concatenate([jnp.where(block == i, a, 0.0) for i in range(PACK)], axis=0)
        both = dot(jnp.concatenate(split(spread), axis=0), basis_of(g))
        fitted = both[: PACK * slots] + both[PACK * slots :]
        for i in range(PACK):
            misfit = pixels_of(PACK * g + i).astype(f32) - fitted[i * slots : (i + 1) * slots]
            square = misfit * misfit
            bundle = 16 * (4 * place[2] + g ^ 7 * place[1]) + 4 * i + 2 * (place[3] & 1) + place[0]
            for half in range(2):
                both = square[2 * half * CAP : 2 * (half + 1) * CAP]
                both = both + square[2 * (half + 2) * CAP : 2 * (half + 3) * CAP]
                parts[half, pl.ds(bundle, 1), :] = jnp.sum(both, axis=0, keepdims=True)
    bands = LANES - 32
    below = groups * CAP
    for half in range(2):
        lines = parts[half].T
        lines = jnp.where(iota(lines.shape, 0) < bands, lines, 0.0)
        energy = jnp.sum(lines, axis=0, keepdims=True) / scale
        energy = jnp.concatenate([energy, jnp.zeros_like(energy)], axis=1)
        for r in (half, half + 2):
            for i in range(2):
                outs[i][r, below:] = jnp.broadcast_to(energy, (8, LANES))


def return_kernel(code, mine, theirs, back1, back2, back3, chosen, energy):
    rows = code.shape[1]
    held, lanes = mine.shape[1] - 8, mine.shape[2]
    backs = (back1, back2, back3)
    tables = [mine.at[0], theirs.at[0]] + [b.at[i] for b in backs for i in range(2)]
    handlers = len(tables)
    wide = lanes // PACK
    codes = code[...]
    pick = one_hot(iota((handlers * held, rows), 0) == codes & 1023)
    table = jnp.concatenate([t[:held] for t in tables], axis=0).T
    found = dot(jnp.concatenate(split(table), axis=0), pick)
    found = found[:lanes] + found[lanes:]
    which = codes >> 10
    result = found[:wide]
    for i in range(1, PACK):
        result = jnp.where(which == i, found[i * wide : (i + 1) * wide], result)
    chosen[...] = result
    total = tables[0][held : held + 1]
    for t in tables[1:]:
        total = total + t[held : held + 1]
    energy[...] = total[:, : energy.shape[1]]


def vmem(shape, dtype):
    return pltpu.VMEM(shape, dtype)


def call(kernel, place, args, outs, scratch, limit, after=()):
    spec = pl.BlockSpec(memory_space=pltpu.VMEM)
    head = [] if place is None else [place]
    return pl.pallas_call(
        kernel,
        out_shape=outs,
        in_specs=[pl.BlockSpec(memory_space=pltpu.SMEM)] * len(head) + [spec] * len(args) + [pl.BlockSpec(memory_space=pl.ANY)] * len(after),
        out_specs=jax.tree.map(lambda _: spec, outs),
        scratch_shapes=scratch,
        compiler_params=pltpu.CompilerParams(vmem_limit_bytes=limit << 20),
    )(*head, *args, *after)


def spots_of(n_blk, n_pix):
    return [(b // 8, b // 2 % 4, b % 2, p // 2, p % 2) for b in range(n_blk) for p in range(n_pix)]


def grouped(spots, key):
    groups = {}
    for index, spot in enumerate(spots):
        groups.setdefault(key(*spot), []).append(index)
    return list(groups.values())


def exchanged(array, groups):
    return lax.all_to_all(array, ALL, 0, 0, tiled=True, axis_index_groups=groups)


def per_device(pixels, bundles, assign):
    rows, bands = pixels.shape
    owned, _, width = bundles.shape
    n_blk, n_pix = lax.axis_size("blk"), lax.axis_size("pix")
    spots = spots_of(n_blk, n_pix)
    column = grouped(spots, lambda z, y, xl, xh, c: (z // 4, xl, xh, c))
    there = {spot: index for index, spot in enumerate(spots)}
    swap = [(there[s], there[(s[0] ^ 7 * s[3],) + s[1:]]) for s in spots]

    def moved(array, r, other):
        pairs = []
        for z, y, xl, xh, c in spots:
            x = (2 * xh + xl + r) % 4
            pairs.append((there[z, y, xl, xh, c], there[z, y, x % 2, x // 2, c ^ other]))
        return lax.ppermute(array, ALL, pairs) if r or other else array

    blk, pix = lax.axis_index("blk"), lax.axis_index("pix")
    z, x_hi = blk >> 3, pix >> 1
    place = jnp.stack([pix & 1, x_hi, z >> 2, 2 * x_hi + (blk & 1)]).astype(jnp.int32)
    sds = jax.ShapeDtypeStruct
    n_col, chips = len(column[0]), 4
    count = n_blk * owned
    groups = n_col // PACK
    held = n_col * CAP

    raw = lax.ppermute(bundles.transpose(0, 2, 1), ALL, swap)
    *sends, code = call(
        slots_kernel,
        place,
        [assign.reshape(1, rows), pixels.T],
        (sds((2, held, LANES), bf16),) * chips + (sds((1, rows), jnp.int32),),
        [vmem((LANES, rows), bf16), vmem((1, rows), f32)],
        16,
    )
    copies = call(
        spread_kernel, place, [raw], sds((n_col, width, LANES), bf16), [vmem((width, LANES), bf16)], 4, [sends[0]]
    )
    gathered = exchanged(copies, column)
    received = [moved(send, r, 0) for r, send in enumerate(sends)]
    theirs = moved(call(stack_kernel, None, received, sds((chips, held, LANES), bf16), [], 8), 0, 1)

    below = groups * CAP
    slots = 2 * chips * CAP
    scale = bands * rows * n_pix / count
    solved = call(
        lambda *refs: solve_kernel(*refs, scale=scale),
        place,
        [gathered, theirs, *received],
        (sds((chips, below + 8, LANES), f32),) * 2,
        [
            vmem((groups, LANES, LANES), bf16),
            vmem((groups, LANES, LANES), bf16),
            vmem((groups, slots, LANES), f32),
            vmem((groups, slots, LANES), f32),
            vmem((groups, LANES), f32),
            vmem((groups, LANES), f32),
            vmem((2, count, LANES), f32),
        ],
        16,
    )
    mine, others = solved[0], moved(solved[1], 0, 1)
    back = [moved(jnp.stack([mine[r], others[r]]), -r, 0) for r in range(1, chips)]
    outs = (sds((width, rows), f32), sds((1, count), f32))
    chosen, energy = call(return_kernel, None, [code, mine, others, *back], outs, [], 16)
    return chosen.T, energy


def solution(mesh):
    placed = (P(("blk", "pix"), None), P("blk", None, None), P(("blk", "pix"), None))
    return jax.shard_map(
        per_device,
        mesh=mesh,
        in_specs=placed,
        out_specs=(P(("blk", "pix"), None), P("blk", None)),
        check_vma=False,
    )
```

```python
import jax
import jax.numpy as jnp
from jax import lax
from jax.experimental import pallas as pl
from jax.experimental.pallas import tpu as pltpu
from jax.sharding import PartitionSpec as P

ITERS = 8
CAP = 16
LANES = 256
ROOT = 0.125
PACK = 4
ALL = ("blk", "pix")
f32, bf16 = jnp.float32, jnp.bfloat16


def iota(shape, dim):
    return lax.broadcasted_iota(jnp.int32, shape, dim)


def one_hot(where):
    return where.astype(f32).astype(bf16)


def split(x):
    high = x.astype(bf16)
    return high, (x - high.astype(f32)).astype(bf16)


def dot(a, b):
    return jnp.dot(a, b, preferred_element_type=f32)


def dot_nt(a, b):
    return lax.dot_general(a, b, (((1,), (1,)), ((), ())), preferred_element_type=f32)


def spread_kernel(place, bundles, after, out, piece, wide, sems):
    bands = bundles.shape[2]
    count = out.shape[0]
    fetch = pltpu.make_async_copy(bundles.at[place[0]], piece, sems.at[count])
    fetch.start()
    wide[...] = jnp.where(iota(wide.shape, 1) == bands, ROOT, 0.0).astype(bf16)
    fetch.wait()
    wide[:, :bands] = piece[...]
    copies = [pltpu.make_async_copy(wide, out.at[i], sems.at[i]) for i in range(count)]
    for copy in copies:
        copy.start()
    for copy in copies:
        copy.wait()


def slots_kernel(place, labels_from, pixels_from, *rest):
    outs, (code, labels, wide, ranks, sems) = rest[:-5], rest[-5:]
    bands, rows = pixels_from.shape
    count = rows // (CAP // 2)
    fetch = pltpu.make_async_copy(labels_from, labels, sems.at[0])
    fetch.start()
    pixels = pltpu.make_async_copy(pixels_from, wide.at[:bands], sems.at[1])
    pixels.start()
    wide[bands:] = jnp.where(iota((LANES - bands, rows), 0) == 0, ROOT, 0.0).astype(bf16)
    fetch.wait()
    label = labels[...]
    chunk = 256
    upper = one_hot(iota((chunk, chunk), 0) <= iota((chunk, chunk), 1))
    carry = jnp.zeros((count, 1), f32)
    for q in range(rows // chunk):
        part = slice(q * chunk, (q + 1) * chunk)
        named = (iota((count, chunk), 0) == label[:, part]).astype(f32)
        running = dot(named.astype(bf16), upper) + carry
        ranks[:, part] = jnp.sum(named * running, axis=0, keepdims=True) - 1.0
        carry = running[:, chunk - 1 :]
    rank = ranks[...].astype(jnp.int32)
    other = (label >> 6) ^ place[2]
    chip = other * 2 + (label >> 1 & 1)
    handler = (chip - place[3] & 3) * 2 + (label + place[0] & 1)
    local = ((label >> 4 & 3) ^ other * 3) * PACK + (label >> 2 & 3)
    slot = local * CAP + rank
    held = outs[0].shape[1]
    pixels.wait()
    for d in range(2 * len(outs)):
        key = jnp.where(handler == d, slot, -1)
        outs[d // 2][d % 2] = dot_nt(one_hot(iota((held, rows), 0) == key), wide[...]).astype(bf16)
    table_row = handler * (held // PACK) + (local >> 2) * CAP + rank
    code[...] = (local & 3) * 1024 + table_row


def stack_kernel(*refs):
    for r, m in enumerate(refs[:-1]):
        refs[-1][r] = m[1]


def blocks():
    return iota((1, LANES), 1) // (LANES // PACK)


def basis_of(bundles, g):
    return jnp.concatenate([bundles[PACK * g + i] for i in range(PACK)], axis=0)


def gram_kernel(bundles, high, low, steps, sums):
    groups = high.shape[0]
    wide = LANES // PACK
    block = blocks()
    same = iota((LANES, LANES), 0) // wide == iota((LANES, LANES), 1) // wide
    for g in range(groups):
        basis = basis_of(bundles, g)
        gram = jnp.where(same, dot_nt(basis, basis), 0.0)
        sums[g : g + 1] = jnp.sum(jnp.abs(gram), axis=0, keepdims=True)
        high[g], low[g] = split(gram)
    total = sums[...]
    largest = jnp.zeros_like(total)
    for i in range(PACK):
        inside = block == i
        largest = jnp.where(inside, jnp.max(jnp.where(inside, total, 0.0), axis=1, keepdims=True), largest)
    steps[...] = 1.0 / largest


def solve_kernel(place, bundles, high, low, steps, theirs, *rest, scale):
    sources = [s for r, m in enumerate(rest[:-5]) for s in (m.at[0], theirs.at[r])]
    outs = rest[-5:-3]
    goal, state, parts = rest[-3:]
    groups = state.shape[0]
    slots = len(sources) * CAP
    block = blocks()

    def pixels_of(local):
        return jnp.concatenate([s[local * CAP : (local + 1) * CAP] for s in sources], axis=0)

    for g in range(groups):
        found = dot_nt(jnp.concatenate([pixels_of(PACK * g + i) for i in range(PACK)], axis=0), basis_of(bundles, g))
        aim = found[:slots]
        for i in range(1, PACK):
            aim = jnp.where(block == i, found[i * slots : (i + 1) * slots], aim)
        goal[g] = aim
    for g in range(groups):
        state[g] = jnp.maximum(steps[g : g + 1] * goal[g], 0.0)

    def sweep(index, carry):
        for g in range(groups):
            a = state[g]
            first, second = split(a)
            both = dot(jnp.concatenate([first, second], axis=0), high[g])
            grad = both[:slots] + both[slots:] + dot(first, low[g])
            state[g] = jnp.maximum(a - steps[g : g + 1] * (grad - goal[g]), 0.0)
        return carry

    lax.fori_loop(1, ITERS, sweep, 0)
    parts[...] = jnp.zeros(parts.shape, f32)
    for g in range(groups):
        a = state[g]
        for s in range(len(sources)):
            outs[s % 2][s // 2, g * CAP : (g + 1) * CAP] = a[s * CAP : (s + 1) * CAP]
        spread = jnp.concatenate([jnp.where(block == i, a, 0.0) for i in range(PACK)], axis=0)
        both = dot(jnp.concatenate(split(spread), axis=0), basis_of(bundles, g))
        fitted = both[: PACK * slots] + both[PACK * slots :]
        for i in range(PACK):
            misfit = pixels_of(PACK * g + i).astype(f32) - fitted[i * slots : (i + 1) * slots]
            square = misfit * misfit
            bundle = 16 * (4 * place[2] + g ^ 7 * place[1]) + 4 * i + 2 * (place[3] & 1) + place[0]
            for half in range(2):
                both = square[2 * half * CAP : 2 * (half + 1) * CAP]
                both = both + square[2 * (half + 2) * CAP : 2 * (half + 3) * CAP]
                parts[half, pl.ds(bundle, 1), :] = jnp.sum(both, axis=0, keepdims=True)
    bands = LANES - 32
    below = groups * CAP
    for half in range(2):
        lines = parts[half].T
        lines = jnp.where(iota(lines.shape, 0) < bands, lines, 0.0)
        energy = jnp.sum(lines, axis=0, keepdims=True) / scale
        energy = jnp.concatenate([energy, jnp.zeros_like(energy)], axis=1)
        for r in (half, half + 2):
            for i in range(2):
                outs[i][r, below:] = jnp.broadcast_to(energy, (8, LANES))


def return_kernel(code, mine, theirs, back1, back2, back3, chosen, energy):
    rows = code.shape[1]
    held, lanes = mine.shape[1] - 8, mine.shape[2]
    backs = (back1, back2, back3)
    tables = [mine.at[0], theirs.at[0]] + [b.at[i] for b in backs for i in range(2)]
    handlers = len(tables)
    wide = lanes // PACK
    codes = code[...]
    pick = one_hot(iota((handlers * held, rows), 0) == codes & 1023)
    table = jnp.concatenate([t[:held] for t in tables], axis=0).T
    found = dot(jnp.concatenate(split(table), axis=0), pick)
    found = found[:lanes] + found[lanes:]
    which = codes >> 10
    result = found[:wide]
    for i in range(1, PACK):
        result = jnp.where(which == i, found[i * wide : (i + 1) * wide], result)
    chosen[...] = result
    total = tables[0][held : held + 1]
    for t in tables[1:]:
        total = total + t[held : held + 1]
    energy[...] = total[:, : energy.shape[1]]


def vmem(shape, dtype):
    return pltpu.VMEM(shape, dtype)


def call(kernel, place, args, outs, scratch, limit, after=(), stays=(), out_stays=False):
    spec, lies = pl.BlockSpec(memory_space=pltpu.VMEM), pl.BlockSpec(memory_space=pl.ANY)
    far = pl.BlockSpec(memory_space=pltpu.HBM)
    head = [] if place is None else [place]
    return pl.pallas_call(
        kernel,
        out_shape=outs,
        in_specs=[pl.BlockSpec(memory_space=pltpu.SMEM)] * len(head)
        + [spec] * len(args)
        + [far] * len(stays)
        + [lies] * len(after),
        out_specs=jax.tree.map(lambda _: far if out_stays else spec, outs),
        scratch_shapes=scratch,
        compiler_params=pltpu.CompilerParams(vmem_limit_bytes=limit << 20),
    )(*head, *args, *stays, *after)


def spots_of(n_blk, n_pix):
    return [(b // 8, b // 2 % 4, b % 2, p // 2, p % 2) for b in range(n_blk) for p in range(n_pix)]


def grouped(spots, key):
    groups = {}
    for index, spot in enumerate(spots):
        groups.setdefault(key(*spot), []).append(index)
    return list(groups.values())


def exchanged(array, groups):
    return lax.all_to_all(array, ALL, 0, 0, tiled=True, axis_index_groups=groups)


def per_device(pixels, bundles, assign):
    rows, bands = pixels.shape
    owned, _, width = bundles.shape
    n_blk, n_pix = lax.axis_size("blk"), lax.axis_size("pix")
    spots = spots_of(n_blk, n_pix)
    column = grouped(spots, lambda z, y, xl, xh, c: (z // 4, xl, xh, c))
    there = {spot: index for index, spot in enumerate(spots)}
    swap = [(there[s], there[(s[0] ^ 7 * s[3],) + s[1:]]) for s in spots]

    def moved(array, r, other):
        pairs = []
        for z, y, xl, xh, c in spots:
            x = (2 * xh + xl + r) % 4
            pairs.append((there[z, y, xl, xh, c], there[z, y, x % 2, x // 2, c ^ other]))
        return lax.ppermute(array, ALL, pairs) if r or other else array

    blk, pix = lax.axis_index("blk"), lax.axis_index("pix")
    z, x_hi = blk >> 3, pix >> 1
    place = jnp.stack([pix & 1, x_hi, z >> 2, 2 * x_hi + (blk & 1)]).astype(jnp.int32)
    sds = jax.ShapeDtypeStruct
    n_col, chips = len(column[0]), 4
    count = n_blk * owned
    groups = n_col // PACK
    held = n_col * CAP

    raw = lax.ppermute(bundles.transpose(0, 2, 1), ALL, swap)
    *sends, code = call(
        slots_kernel,
        place,
        [],
        (sds((2, held, LANES), bf16),) * chips + (sds((1, rows), jnp.int32),),
        [vmem((1, rows), jnp.int32), vmem((LANES, rows), bf16), vmem((1, rows), f32), pltpu.SemaphoreType.DMA((2,))],
        16,
        stays=[assign.reshape(1, rows), pixels.T],
    )
    copies = call(
        spread_kernel,
        place,
        [],
        sds((n_col, width, LANES), bf16),
        [vmem((width, bands), bf16), vmem((width, LANES), bf16), pltpu.SemaphoreType.DMA((n_col + 1,))],
        4,
        stays=[raw],
        after=[sends[0]],
        out_stays=True,
    )
    gathered = exchanged(copies, column)
    received = [moved(send, r, 0) for r, send in enumerate(sends)]
    theirs = moved(call(stack_kernel, None, received, sds((chips, held, LANES), bf16), [], 8), 0, 1)

    below = groups * CAP
    slots = 2 * chips * CAP
    scale = bands * rows * n_pix / count
    square = sds((groups, LANES, LANES), bf16)
    grams = call(
        gram_kernel,
        None,
        [gathered],
        (square, square, sds((groups, LANES), f32)),
        [vmem((groups, LANES), f32)],
        16,
    )
    solved = call(
        lambda *refs: solve_kernel(*refs, scale=scale),
        place,
        [gathered, *grams, theirs, *received],
        (sds((chips, below + 8, LANES), f32),) * 2,
        [
            vmem((groups, slots, LANES), f32),
            vmem((groups, slots, LANES), f32),
            vmem((2, count, LANES), f32),
        ],
        16,
    )
    mine, others = solved[0], moved(solved[1], 0, 1)
    back = [moved(jnp.stack([mine[r], others[r]]), -r, 0) for r in range(1, chips)]
    outs = (sds((width, rows), f32), sds((1, count), f32))
    chosen, energy = call(return_kernel, None, [code, mine, others, *back], outs, [], 16)
    return chosen.T, energy


def solution(mesh):
    placed = (P(("blk", "pix"), None), P("blk", None, None), P(("blk", "pix"), None))
    return jax.shard_map(
        per_device,
        mesh=mesh,
        in_specs=placed,
        out_specs=(P(("blk", "pix"), None), P("blk", None)),
        check_vma=False,
    )
```

```python
import jax
import jax.numpy as jnp
from jax import lax
from jax.experimental import pallas as pl
from jax.experimental.pallas import tpu as pltpu
from jax.sharding import PartitionSpec as P

ITERS = 8
CAP = 16
LANES = 256
ROOT = 0.125
PACK = 4
ALL = ("blk", "pix")
f32, bf16 = jnp.float32, jnp.bfloat16


def iota(shape, dim):
    return lax.broadcasted_iota(jnp.int32, shape, dim)


def one_hot(where):
    return where.astype(f32).astype(bf16)


def split(x):
    high = x.astype(bf16)
    return high, (x - high.astype(f32)).astype(bf16)


def dot(a, b):
    return jnp.dot(a, b, preferred_element_type=f32)


def dot_nt(a, b):
    return lax.dot_general(a, b, (((1,), (1,)), ((), ())), preferred_element_type=f32)


def prep_kernel(place, bundles, *rest):
    out = rest[-1]
    bands = bundles.shape[2]
    out[...] = jnp.where(iota(out.shape, 1) == bands, ROOT, 0.0).astype(bf16)
    out[:, :bands] = bundles[place[0]]


def slots_kernel(place, labels, pixels, *rest):
    outs, (code, wide, ranks) = rest[:-3], rest[-3:]
    bands, rows = pixels.shape
    count = rows // (CAP // 2)
    wide[:bands] = pixels[...]
    wide[bands:] = jnp.where(iota((LANES - bands, rows), 0) == 0, ROOT, 0.0).astype(bf16)
    label = labels[...]
    chunk = 256
    upper = one_hot(iota((chunk, chunk), 0) <= iota((chunk, chunk), 1))
    carry = jnp.zeros((count, 1), f32)
    for q in range(rows // chunk):
        part = slice(q * chunk, (q + 1) * chunk)
        named = (iota((count, chunk), 0) == label[:, part]).astype(f32)
        running = dot(named.astype(bf16), upper) + carry
        ranks[:, part] = jnp.sum(named * running, axis=0, keepdims=True) - 1.0
        carry = running[:, chunk - 1 :]
    rank = ranks[...].astype(jnp.int32)
    other = (label >> 6) ^ (place[2] >> 2)
    chip = other * 2 + (label >> 1 & 1)
    handler = (chip - place[3] & 3) * 2 + (label + place[0] & 1)
    local = (place[2] - ((label >> 4) ^ other * 3) & 3) * PACK + (place[4] - (label >> 2) & 3)
    slot = local * CAP + rank
    held = outs[0].shape[1]
    for d in range(2 * len(outs)):
        key = jnp.where(handler == d, slot, -1)
        outs[d // 2][d % 2] = dot_nt(one_hot(iota((held, rows), 0) == key), wide[...]).astype(bf16)
    table_row = handler * (held // PACK) + (local >> 2) * CAP + rank
    code[...] = (local & 3) * 1024 + table_row


def stack_kernel(*refs):
    for r, m in enumerate(refs[: refs[-1].shape[0]]):
        refs[-1][r] = m[1]


def blocks():
    return iota((1, LANES), 1) // (LANES // PACK)


def basis_of(bundles, g):
    return jnp.concatenate([b[g] for b in bundles], axis=0)


def gram_kernel(*refs):
    bundles, (high, low, steps, sums) = refs[:-4], refs[-4:]
    groups = high.shape[0]
    wide = LANES // PACK
    block = blocks()
    same = iota((LANES, LANES), 0) // wide == iota((LANES, LANES), 1) // wide
    for g in range(groups):
        basis = basis_of(bundles, g)
        gram = jnp.where(same, dot_nt(basis, basis), 0.0)
        sums[g : g + 1] = jnp.sum(jnp.abs(gram), axis=0, keepdims=True)
        high[g], low[g] = split(gram)
    total = sums[...]
    largest = jnp.zeros_like(total)
    for i in range(PACK):
        inside = block == i
        largest = jnp.where(inside, jnp.max(jnp.where(inside, total, 0.0), axis=1, keepdims=True), largest)
    steps[...] = 1.0 / largest


def solve_kernel(place, *refs, scale):
    bundles, (high, low, steps, theirs, *rest) = refs[:PACK], refs[PACK:]
    sources = [s for r, m in enumerate(rest[:-5]) for s in (m.at[0], theirs.at[r])]
    outs = rest[-5:-3]
    goal, state, parts = rest[-3:]
    groups = state.shape[0]
    slots = len(sources) * CAP
    block = blocks()

    def pixels_of(local):
        return jnp.concatenate([s[local * CAP : (local + 1) * CAP] for s in sources], axis=0)

    for g in range(groups):
        found = dot_nt(jnp.concatenate([pixels_of(PACK * g + i) for i in range(PACK)], axis=0), basis_of(bundles, g))
        aim = found[:slots]
        for i in range(1, PACK):
            aim = jnp.where(block == i, found[i * slots : (i + 1) * slots], aim)
        goal[g] = aim
    for g in range(groups):
        state[g] = jnp.maximum(steps[g : g + 1] * goal[g], 0.0)

    def sweep(index, carry):
        for g in range(groups):
            a = state[g]
            first, second = split(a)
            both = dot(jnp.concatenate([first, second], axis=0), high[g])
            grad = both[:slots] + both[slots:] + dot(first, low[g])
            state[g] = jnp.maximum(a - steps[g : g + 1] * (grad - goal[g]), 0.0)
        return carry

    lax.fori_loop(1, ITERS, sweep, 0)
    parts[...] = jnp.zeros(parts.shape, f32)
    for g in range(groups):
        a = state[g]
        for s in range(len(sources)):
            outs[s % 2][s // 2, g * CAP : (g + 1) * CAP] = a[s * CAP : (s + 1) * CAP]
        spread = jnp.concatenate([jnp.where(block == i, a, 0.0) for i in range(PACK)], axis=0)
        both = dot(jnp.concatenate(split(spread), axis=0), basis_of(bundles, g))
        fitted = both[: PACK * slots] + both[PACK * slots :]
        for i in range(PACK):
            misfit = pixels_of(PACK * g + i).astype(f32) - fitted[i * slots : (i + 1) * slots]
            square = misfit * misfit
            z, y = (place[2] & 4) + (place[2] - g & 3) ^ 7 * place[1], place[4] - i & 3
            bundle = 16 * z + 4 * y + 2 * (place[3] & 1) + place[0]
            for half in range(2):
                both = square[2 * half * CAP : 2 * (half + 1) * CAP]
                both = both + square[2 * (half + 2) * CAP : 2 * (half + 3) * CAP]
                parts[half, pl.ds(bundle, 1), :] = jnp.sum(both, axis=0, keepdims=True)
    bands = LANES - 32
    below = groups * CAP
    for half in range(2):
        lines = parts[half].T
        lines = jnp.where(iota(lines.shape, 0) < bands, lines, 0.0)
        energy = jnp.sum(lines, axis=0, keepdims=True) / scale
        energy = jnp.concatenate([energy, jnp.zeros_like(energy)], axis=1)
        for r in (half, half + 2):
            for i in range(2):
                outs[i][r, below:] = jnp.broadcast_to(energy, (8, LANES))


def return_kernel(code, mine, theirs, back1, back2, back3, chosen, energy):
    rows = code.shape[1]
    held, lanes = mine.shape[1] - 8, mine.shape[2]
    backs = (back1, back2, back3)
    tables = [mine.at[0], theirs.at[0]] + [b.at[i] for b in backs for i in range(2)]
    handlers = len(tables)
    wide = lanes // PACK
    codes = code[...]
    pick = one_hot(iota((handlers * held, rows), 0) == codes & 1023)
    table = jnp.concatenate([t[:held] for t in tables], axis=0).T
    found = dot(jnp.concatenate(split(table), axis=0), pick)
    found = found[:lanes] + found[lanes:]
    which = codes >> 10
    result = found[:wide]
    for i in range(1, PACK):
        result = jnp.where(which == i, found[i * wide : (i + 1) * wide], result)
    chosen[...] = result
    total = tables[0][held : held + 1]
    for t in tables[1:]:
        total = total + t[held : held + 1]
    energy[...] = total[:, : energy.shape[1]]


def vmem(shape, dtype):
    return pltpu.VMEM(shape, dtype)


def call(kernel, place, args, outs, scratch, limit, after=()):
    spec = pl.BlockSpec(memory_space=pltpu.VMEM)
    head = [] if place is None else [place]
    return pl.pallas_call(
        kernel,
        out_shape=outs,
        in_specs=[pl.BlockSpec(memory_space=pltpu.SMEM)] * len(head) + [spec] * len(args) + [pl.BlockSpec(memory_space=pl.ANY)] * len(after),
        out_specs=jax.tree.map(lambda _: spec, outs),
        scratch_shapes=scratch,
        compiler_params=pltpu.CompilerParams(vmem_limit_bytes=limit << 20),
    )(*head, *args, *after)


def spots_of(n_blk, n_pix):
    return [(b // 8, b // 2 % 4, b % 2, p // 2, p % 2) for b in range(n_blk) for p in range(n_pix)]


def per_device(pixels, bundles, assign):
    rows, bands = pixels.shape
    owned, _, width = bundles.shape
    n_blk, n_pix = lax.axis_size("blk"), lax.axis_size("pix")
    spots = spots_of(n_blk, n_pix)
    there = {spot: index for index, spot in enumerate(spots)}

    def sent(array, target):
        return lax.ppermute(array, ALL, [(there[s], there[target(*s)]) for s in spots])

    def along_x(array, r):
        def target(z, y, xl, xh, c):
            x = 2 * xh + xl + r & 3
            return z, y, x & 1, x >> 1, c

        return sent(array, target) if r else array

    def to_sibling(array):
        return sent(array, lambda z, y, xl, xh, c: (z, y, xl, xh, c ^ 1))

    blk, pix = lax.axis_index("blk"), lax.axis_index("pix")
    z, x_hi = blk >> 3, pix >> 1
    place = jnp.stack([pix & 1, x_hi, z, 2 * x_hi + (blk & 1), blk >> 1 & 3]).astype(jnp.int32)
    sds = jax.ShapeDtypeStruct
    chips = 4
    count = n_blk * owned
    groups = 4
    held = groups * PACK * CAP

    *sends, code = call(
        slots_kernel,
        place,
        [assign.reshape(1, rows), pixels.T],
        (sds((2, held, LANES), bf16),) * chips + (sds((1, rows), jnp.int32),),
        [vmem((LANES, rows), bf16), vmem((1, rows), f32)],
        16,
    )
    received = [along_x(send, r) for r, send in enumerate(sends)]
    basis = call(prep_kernel, place, [bundles.transpose(0, 2, 1)], sds((width, LANES), bf16), [], 4)
    pieces = []
    for q in range(groups):

        def around(z, y, xl, xh, c):
            held = z ^ 7 * xh
            return held & 4 | held + q & 3, y, xl, xh, c

        pieces.append(sent(basis, around))
    levels = jnp.stack(pieces)
    gathered = [levels]
    for r in range(1, PACK):
        gathered.append(sent(levels, lambda z, y, xl, xh, c: (z, y + r & 3, xl, xh, c)))
    stacked = call(stack_kernel, None, received, sds((chips, held, LANES), bf16), [], 8, gathered[1:])
    theirs = to_sibling(stacked)

    below = groups * CAP
    slots = 2 * chips * CAP
    scale = bands * rows * n_pix / count
    square = sds((groups, LANES, LANES), bf16)
    grams = call(
        gram_kernel,
        None,
        gathered,
        (square, square, sds((groups, LANES), f32)),
        [vmem((groups, LANES), f32)],
        16,
    )
    solved = call(
        lambda *refs: solve_kernel(*refs, scale=scale),
        place,
        [*gathered, *grams, theirs, *received],
        (sds((chips, below + 8, LANES), f32),) * 2,
        [
            vmem((groups, slots, LANES), f32),
            vmem((groups, slots, LANES), f32),
            vmem((2, count, LANES), f32),
        ],
        16,
    )
    mine, others = solved[0], to_sibling(solved[1])
    back = [along_x(jnp.stack([mine[r], others[r]]), -r) for r in range(1, chips)]
    outs = (sds((width, rows), f32), sds((1, count), f32))
    chosen, energy = call(return_kernel, None, [code, mine, others, *back], outs, [], 16)
    return chosen.T, energy


def solution(mesh):
    placed = (P(("blk", "pix"), None), P("blk", None, None), P(("blk", "pix"), None))
    return jax.shard_map(
        per_device,
        mesh=mesh,
        in_specs=placed,
        out_specs=(P(("blk", "pix"), None), P("blk", None)),
        check_vma=False,
    )
```

```python
import jax
import jax.numpy as jnp
from jax import lax
from jax.experimental import pallas as pl
from jax.experimental.pallas import tpu as pltpu
from jax.sharding import PartitionSpec as P

ITERS = 8
CAP = 16
LANES = 256
ROOT = 0.125
PACK = 4
ALL = ("blk", "pix")
f32, bf16 = jnp.float32, jnp.bfloat16


def iota(shape, dim):
    return lax.broadcasted_iota(jnp.int32, shape, dim)


def one_hot(where):
    return where.astype(f32).astype(bf16)


def split(x):
    high = x.astype(bf16)
    return high, (x - high.astype(f32)).astype(bf16)


def dot(a, b):
    return jnp.dot(a, b, preferred_element_type=f32)


def dot_nt(a, b):
    return lax.dot_general(a, b, (((1,), (1,)), ((), ())), preferred_element_type=f32)


def prep_kernel(place, bundles, *rest):
    out = rest[-1]
    bands = bundles.shape[2]
    out[...] = jnp.where(iota(out.shape, 1) == bands, ROOT, 0.0).astype(bf16)
    out[:, :bands] = bundles[place[0]]


def slots_kernel(place, labels, pixels, *rest):
    outs, (code, wide, ranks) = rest[:-3], rest[-3:]
    bands, rows = pixels.shape
    count = rows // (CAP // 2)
    wide[:bands] = pixels[...]
    wide[bands:] = jnp.where(iota((LANES - bands, rows), 0) == 0, ROOT, 0.0).astype(bf16)
    label = labels[...]
    chunk = 256
    upper = one_hot(iota((chunk, chunk), 0) <= iota((chunk, chunk), 1))
    carry = jnp.zeros((count, 1), f32)
    for q in range(rows // chunk):
        part = slice(q * chunk, (q + 1) * chunk)
        named = (iota((count, chunk), 0) == label[:, part]).astype(f32)
        running = dot(named.astype(bf16), upper) + carry
        ranks[:, part] = jnp.sum(named * running, axis=0, keepdims=True) - 1.0
        carry = running[:, chunk - 1 :]
    rank = ranks[...].astype(jnp.int32)
    other = (label >> 6) ^ (place[2] >> 2)
    chip = other * 2 + (label >> 1 & 1)
    handler = (chip - place[3] & 3) * 2 + (label + place[0] & 1)
    local = (place[2] - ((label >> 4) ^ other * 3) & 3) * PACK + (place[4] - (label >> 2) & 3)
    slot = local * CAP + rank
    held = outs[0].shape[1]
    for d in range(2 * len(outs)):
        key = jnp.where(handler == d, slot, -1)
        outs[d // 2][d % 2] = dot_nt(one_hot(iota((held, rows), 0) == key), wide[...]).astype(bf16)
    table_row = handler * (held // PACK) + (local >> 2) * CAP + rank
    code[...] = (local & 3) * 1024 + table_row


def stack_kernel(*refs):
    for r, m in enumerate(refs[: refs[-1].shape[0]]):
        refs[-1][r] = m[1]


def blocks():
    return iota((1, LANES), 1) // (LANES // PACK)


def basis_of(bundles, g):
    return jnp.concatenate([b[g] for b in bundles], axis=0)


def gram_kernel(*refs):
    bundles, (high, low, steps, sums) = refs[:-4], refs[-4:]
    groups = high.shape[0]
    wide = LANES // PACK
    block = blocks()
    same = iota((LANES, LANES), 0) // wide == iota((LANES, LANES), 1) // wide
    for g in range(groups):
        basis = basis_of(bundles, g)
        gram = jnp.where(same, dot_nt(basis, basis), 0.0)
        sums[g : g + 1] = jnp.sum(jnp.abs(gram), axis=0, keepdims=True)
        high[g], low[g] = split(gram)
    total = sums[...]
    largest = jnp.zeros_like(total)
    for i in range(PACK):
        inside = block == i
        largest = jnp.where(inside, jnp.max(jnp.where(inside, total, 0.0), axis=1, keepdims=True), largest)
    steps[...] = 1.0 / largest


def solve_kernel(place, *refs, scale):
    bundles, (high, low, steps, theirs, *rest) = refs[:PACK], refs[PACK:]
    sources = [s for r, m in enumerate(rest[:-5]) for s in (m.at[0], theirs.at[r])]
    outs = rest[-5:-3]
    goal, state, parts = rest[-3:]
    groups = state.shape[0]
    slots = len(sources) * CAP
    block = blocks()

    def pixels_of(local):
        return jnp.concatenate([s[local * CAP : (local + 1) * CAP] for s in sources], axis=0)

    for g in range(groups):
        found = dot_nt(jnp.concatenate([pixels_of(PACK * g + i) for i in range(PACK)], axis=0), basis_of(bundles, g))
        aim = found[:slots]
        for i in range(1, PACK):
            aim = jnp.where(block == i, found[i * slots : (i + 1) * slots], aim)
        goal[g] = aim
    for g in range(groups):
        state[g] = jnp.maximum(steps[g : g + 1] * goal[g], 0.0)

    def sweep(index, carry):
        for g in range(groups):
            a = state[g]
            first, second = split(a)
            both = dot(jnp.concatenate([first, second], axis=0), high[g])
            grad = both[:slots] + both[slots:] + dot(first, low[g])
            state[g] = jnp.maximum(a - steps[g : g + 1] * (grad - goal[g]), 0.0)
        return carry

    lax.fori_loop(1, ITERS, sweep, 0, unroll=True)
    parts[...] = jnp.zeros(parts.shape, f32)
    for g in range(groups):
        a = state[g]
        for s in range(len(sources)):
            outs[s % 2][s // 2, g * CAP : (g + 1) * CAP] = a[s * CAP : (s + 1) * CAP]
        spread = jnp.concatenate([jnp.where(block == i, a, 0.0) for i in range(PACK)], axis=0)
        both = dot(jnp.concatenate(split(spread), axis=0), basis_of(bundles, g))
        fitted = both[: PACK * slots] + both[PACK * slots :]
        for i in range(PACK):
            misfit = pixels_of(PACK * g + i).astype(f32) - fitted[i * slots : (i + 1) * slots]
            square = misfit * misfit
            z, y = (place[2] & 4) + (place[2] - g & 3) ^ 7 * place[1], place[4] - i & 3
            bundle = 16 * z + 4 * y + 2 * (place[3] & 1) + place[0]
            for half in range(2):
                both = square[2 * half * CAP : 2 * (half + 1) * CAP]
                both = both + square[2 * (half + 2) * CAP : 2 * (half + 3) * CAP]
                parts[half, pl.ds(bundle, 1), :] = jnp.sum(both, axis=0, keepdims=True)
    bands = LANES - 32
    below = groups * CAP
    for half in range(2):
        lines = parts[half].T
        lines = jnp.where(iota(lines.shape, 0) < bands, lines, 0.0)
        energy = jnp.sum(lines, axis=0, keepdims=True) / scale
        energy = jnp.concatenate([energy, jnp.zeros_like(energy)], axis=1)
        for r in (half, half + 2):
            for i in range(2):
                outs[i][r, below:] = jnp.broadcast_to(energy, (8, LANES))


def return_kernel(code, mine, theirs, back1, back2, back3, chosen, energy):
    rows = code.shape[1]
    held, lanes = mine.shape[1] - 8, mine.shape[2]
    backs = (back1, back2, back3)
    tables = [mine.at[0], theirs.at[0]] + [b.at[i] for b in backs for i in range(2)]
    handlers = len(tables)
    wide = lanes // PACK
    codes = code[...]
    pick = one_hot(iota((handlers * held, rows), 0) == codes & 1023)
    table = jnp.concatenate([t[:held] for t in tables], axis=0).T
    found = dot(jnp.concatenate(split(table), axis=0), pick)
    found = found[:lanes] + found[lanes:]
    which = codes >> 10
    result = found[:wide]
    for i in range(1, PACK):
        result = jnp.where(which == i, found[i * wide : (i + 1) * wide], result)
    chosen[...] = result
    total = tables[0][held : held + 1]
    for t in tables[1:]:
        total = total + t[held : held + 1]
    energy[...] = total[:, : energy.shape[1]]


def vmem(shape, dtype):
    return pltpu.VMEM(shape, dtype)


def call(kernel, place, args, outs, scratch, limit, after=()):
    spec = pl.BlockSpec(memory_space=pltpu.VMEM)
    head = [] if place is None else [place]
    return pl.pallas_call(
        kernel,
        out_shape=outs,
        in_specs=[pl.BlockSpec(memory_space=pltpu.SMEM)] * len(head) + [spec] * len(args) + [pl.BlockSpec(memory_space=pl.ANY)] * len(after),
        out_specs=jax.tree.map(lambda _: spec, outs),
        scratch_shapes=scratch,
        compiler_params=pltpu.CompilerParams(vmem_limit_bytes=limit << 20),
    )(*head, *args, *after)


def spots_of(n_blk, n_pix):
    return [(b // 8, b // 2 % 4, b % 2, p // 2, p % 2) for b in range(n_blk) for p in range(n_pix)]


def per_device(pixels, bundles, assign):
    rows, bands = pixels.shape
    owned, _, width = bundles.shape
    n_blk, n_pix = lax.axis_size("blk"), lax.axis_size("pix")
    spots = spots_of(n_blk, n_pix)
    there = {spot: index for index, spot in enumerate(spots)}

    def sent(array, target):
        return lax.ppermute(array, ALL, [(there[s], there[target(*s)]) for s in spots])

    def along_x(array, r):
        def target(z, y, xl, xh, c):
            x = 2 * xh + xl + r & 3
            return z, y, x & 1, x >> 1, c

        return sent(array, target) if r else array

    def to_sibling(array):
        return sent(array, lambda z, y, xl, xh, c: (z, y, xl, xh, c ^ 1))

    blk, pix = lax.axis_index("blk"), lax.axis_index("pix")
    z, x_hi = blk >> 3, pix >> 1
    place = jnp.stack([pix & 1, x_hi, z, 2 * x_hi + (blk & 1), blk >> 1 & 3]).astype(jnp.int32)
    sds = jax.ShapeDtypeStruct
    chips = 4
    count = n_blk * owned
    groups = 4
    held = groups * PACK * CAP

    *sends, code = call(
        slots_kernel,
        place,
        [assign.reshape(1, rows), pixels.T],
        (sds((2, held, LANES), bf16),) * chips + (sds((1, rows), jnp.int32),),
        [vmem((LANES, rows), bf16), vmem((1, rows), f32)],
        16,
    )
    received = [along_x(send, r) for r, send in enumerate(sends)]
    basis = call(prep_kernel, place, [bundles.transpose(0, 2, 1)], sds((width, LANES), bf16), [], 4, [sends[0]])
    pieces = []
    for q in range(groups):

        def around(z, y, xl, xh, c):
            held = z ^ 7 * xh
            return held & 4 | held + q & 3, y, xl, xh, c

        pieces.append(sent(basis, around))
    levels = jnp.stack(pieces)
    gathered = [levels]
    for r in range(1, PACK):
        gathered.append(sent(levels, lambda z, y, xl, xh, c: (z, y + r & 3, xl, xh, c)))
    stacked = call(stack_kernel, None, received, sds((chips, held, LANES), bf16), [], 8, gathered[1:])
    theirs = to_sibling(stacked)

    below = groups * CAP
    slots = 2 * chips * CAP
    scale = bands * rows * n_pix / count
    square = sds((groups, LANES, LANES), bf16)
    grams = call(
        gram_kernel,
        None,
        gathered,
        (square, square, sds((groups, LANES), f32)),
        [vmem((groups, LANES), f32)],
        16,
    )
    solved = call(
        lambda *refs: solve_kernel(*refs, scale=scale),
        place,
        [*gathered, *grams, theirs, *received],
        (sds((chips, below + 8, LANES), f32),) * 2,
        [
            vmem((groups, slots, LANES), f32),
            vmem((groups, slots, LANES), f32),
            vmem((2, count, LANES), f32),
        ],
        16,
    )
    mine, others = solved[0], to_sibling(solved[1])
    back = [along_x(jnp.stack([mine[r], others[r]]), -r) for r in range(1, chips)]
    outs = (sds((width, rows), f32), sds((1, count), f32))
    chosen, energy = call(return_kernel, None, [code, mine, others, *back], outs, [], 16)
    return chosen.T, energy


def solution(mesh):
    placed = (P(("blk", "pix"), None), P("blk", None, None), P(("blk", "pix"), None))
    return jax.shard_map(
        per_device,
        mesh=mesh,
        in_specs=placed,
        out_specs=(P(("blk", "pix"), None), P("blk", None)),
        check_vma=False,
    )
```

```python
import jax
import jax.numpy as jnp
from jax import lax
from jax.experimental import pallas as pl
from jax.experimental.pallas import tpu as pltpu
from jax.sharding import PartitionSpec as P

ITERS = 8
CAP = 16
LANES = 256
ROOT = 0.125
PACK = 4
ALL = ("blk", "pix")
f32, bf16 = jnp.float32, jnp.bfloat16


def iota(shape, dim):
    return lax.broadcasted_iota(jnp.int32, shape, dim)


def one_hot(where):
    return where.astype(f32).astype(bf16)


def split(x):
    high = x.astype(bf16)
    return high, (x - high.astype(f32)).astype(bf16)


def dot(a, b):
    return jnp.dot(a, b, preferred_element_type=f32)


def dot_nt(a, b):
    return lax.dot_general(a, b, (((1,), (1,)), ((), ())), preferred_element_type=f32)


def spread_kernel(place, bundles, *rest):
    out, wide = rest[-2:]
    bands = bundles.shape[2]
    wide[...] = jnp.where(iota(wide.shape, 1) == bands, ROOT, 0.0).astype(bf16)
    wide[:, :bands] = bundles[place[0]]
    for i in range(out.shape[0]):
        out[i] = wide[...]


def slots_kernel(place, labels, pixels, *rest):
    outs, (code, wide, ranks) = rest[:-3], rest[-3:]
    bands, rows = pixels.shape
    count = rows // (CAP // 2)
    wide[:bands] = pixels[...]
    wide[bands:] = jnp.where(iota((LANES - bands, rows), 0) == 0, ROOT, 0.0).astype(bf16)
    label = labels[...]
    chunk = 256
    upper = one_hot(iota((chunk, chunk), 0) <= iota((chunk, chunk), 1))
    carry = jnp.zeros((count, 1), f32)
    for q in range(rows // chunk):
        part = slice(q * chunk, (q + 1) * chunk)
        named = (iota((count, chunk), 0) == label[:, part]).astype(f32)
        running = dot(named.astype(bf16), upper) + carry
        ranks[:, part] = jnp.sum(named * running, axis=0, keepdims=True) - 1.0
        carry = running[:, chunk - 1 :]
    rank = ranks[...].astype(jnp.int32)
    other = (label >> 6) ^ place[2]
    chip = other * 2 + (label >> 1 & 1)
    handler = (chip - place[3] & 3) * 2 + (label + place[0] & 1)
    local = ((label >> 4 & 3) ^ other * 3) * PACK + (label >> 2 & 3)
    slot = local * CAP + rank
    held = outs[0].shape[1]
    for d in range(2 * len(outs)):
        key = jnp.where(handler == d, slot, -1)
        outs[d // 2][d % 2] = dot_nt(one_hot(iota((held, rows), 0) == key), wide[...]).astype(bf16)
    table_row = handler * (held // PACK) + (local >> 2) * CAP + rank
    code[...] = (local & 3) * 1024 + table_row


def stack_kernel(*refs):
    for r, m in enumerate(refs[:-1]):
        refs[-1][r] = m[1]


def blocks():
    return iota((1, LANES), 1) // (LANES // PACK)


def basis_of(bundles, g):
    return jnp.concatenate([bundles[PACK * g + i] for i in range(PACK)], axis=0)


def gram_kernel(bundles, high, low, steps, sums):
    groups = high.shape[0]
    wide = LANES // PACK
    block = blocks()
    same = iota((LANES, LANES), 0) // wide == iota((LANES, LANES), 1) // wide
    for g in range(groups):
        basis = basis_of(bundles, g)
        gram = jnp.where(same, dot_nt(basis, basis), 0.0)
        sums[g : g + 1] = jnp.sum(jnp.abs(gram), axis=0, keepdims=True)
        high[g], low[g] = split(gram)
    total = sums[...]
    largest = jnp.zeros_like(total)
    for i in range(PACK):
        inside = block == i
        largest = jnp.where(inside, jnp.max(jnp.where(inside, total, 0.0), axis=1, keepdims=True), largest)
    steps[...] = 1.0 / largest


def solve_kernel(place, bundles, high, low, steps, theirs, *rest, scale):
    sources = [s for r, m in enumerate(rest[:-5]) for s in (m.at[0], theirs.at[r])]
    outs = rest[-5:-3]
    goal, state, parts = rest[-3:]
    groups = state.shape[0]
    slots = len(sources) * CAP
    block = blocks()

    def pixels_of(local):
        return jnp.concatenate([s[local * CAP : (local + 1) * CAP] for s in sources], axis=0)

    for g in range(groups):
        found = dot_nt(jnp.concatenate([pixels_of(PACK * g + i) for i in range(PACK)], axis=0), basis_of(bundles, g))
        aim = found[:slots]
        for i in range(1, PACK):
            aim = jnp.where(block == i, found[i * slots : (i + 1) * slots], aim)
        goal[g] = aim
    for g in range(groups):
        state[g] = jnp.maximum(steps[g : g + 1] * goal[g], 0.0)

    def sweep(index, carry):
        for g in range(groups):
            a = state[g]
            first, second = split(a)
            both = dot(jnp.concatenate([first, second], axis=0), high[g])
            grad = both[:slots] + both[slots:] + dot(first, low[g])
            state[g] = jnp.maximum(a - steps[g : g + 1] * (grad - goal[g]), 0.0)
        return carry

    lax.fori_loop(1, ITERS, sweep, 0, unroll=True)
    parts[...] = jnp.zeros(parts.shape, f32)
    for g in range(groups):
        a = state[g]
        for s in range(len(sources)):
            outs[s % 2][s // 2, g * CAP : (g + 1) * CAP] = a[s * CAP : (s + 1) * CAP]
        spread = jnp.concatenate([jnp.where(block == i, a, 0.0) for i in range(PACK)], axis=0)
        both = dot(jnp.concatenate(split(spread), axis=0), basis_of(bundles, g))
        fitted = both[: PACK * slots] + both[PACK * slots :]
        for i in range(PACK):
            misfit = pixels_of(PACK * g + i).astype(f32) - fitted[i * slots : (i + 1) * slots]
            square = misfit * misfit
            bundle = 16 * (4 * place[2] + g ^ 7 * place[1]) + 4 * i + 2 * (place[3] & 1) + place[0]
            for half in range(2):
                both = square[2 * half * CAP : 2 * (half + 1) * CAP]
                both = both + square[2 * (half + 2) * CAP : 2 * (half + 3) * CAP]
                parts[half, pl.ds(bundle, 1), :] = jnp.sum(both, axis=0, keepdims=True)
    bands = LANES - 32
    below = groups * CAP
    for half in range(2):
        lines = parts[half].T
        lines = jnp.where(iota(lines.shape, 0) < bands, lines, 0.0)
        energy = jnp.sum(lines, axis=0, keepdims=True) / scale
        energy = jnp.concatenate([energy, jnp.zeros_like(energy)], axis=1)
        for r in (half, half + 2):
            for i in range(2):
                outs[i][r, below:] = jnp.broadcast_to(energy, (8, LANES))


def return_kernel(code, mine, theirs, back1, back2, back3, chosen, energy):
    rows = code.shape[1]
    held, lanes = mine.shape[1] - 8, mine.shape[2]
    backs = (back1, back2, back3)
    tables = [mine.at[0], theirs.at[0]] + [b.at[i] for b in backs for i in range(2)]
    handlers = len(tables)
    wide = lanes // PACK
    codes = code[...]
    pick = one_hot(iota((handlers * held, rows), 0) == codes & 1023)
    table = jnp.concatenate([t[:held] for t in tables], axis=0).T
    found = dot(jnp.concatenate(split(table), axis=0), pick)
    found = found[:lanes] + found[lanes:]
    which = codes >> 10
    result = found[:wide]
    for i in range(1, PACK):
        result = jnp.where(which == i, found[i * wide : (i + 1) * wide], result)
    chosen[...] = result
    total = tables[0][held : held + 1]
    for t in tables[1:]:
        total = total + t[held : held + 1]
    energy[...] = total[:, : energy.shape[1]]


def vmem(shape, dtype):
    return pltpu.VMEM(shape, dtype)


def call(kernel, place, args, outs, scratch, limit, after=()):
    spec = pl.BlockSpec(memory_space=pltpu.VMEM)
    head = [] if place is None else [place]
    return pl.pallas_call(
        kernel,
        out_shape=outs,
        in_specs=[pl.BlockSpec(memory_space=pltpu.SMEM)] * len(head) + [spec] * len(args) + [pl.BlockSpec(memory_space=pl.ANY)] * len(after),
        out_specs=jax.tree.map(lambda _: spec, outs),
        scratch_shapes=scratch,
        compiler_params=pltpu.CompilerParams(vmem_limit_bytes=limit << 20),
    )(*head, *args, *after)


def spots_of(n_blk, n_pix):
    return [(b // 8, b // 2 % 4, b % 2, p // 2, p % 2) for b in range(n_blk) for p in range(n_pix)]


def grouped(spots, key):
    groups = {}
    for index, spot in enumerate(spots):
        groups.setdefault(key(*spot), []).append(index)
    return list(groups.values())


def exchanged(array, groups):
    return lax.all_to_all(array, ALL, 0, 0, tiled=True, axis_index_groups=groups)


def per_device(pixels, bundles, assign):
    rows, bands = pixels.shape
    owned, _, width = bundles.shape
    n_blk, n_pix = lax.axis_size("blk"), lax.axis_size("pix")
    spots = spots_of(n_blk, n_pix)
    column = grouped(spots, lambda z, y, xl, xh, c: (z // 4, xl, xh, c))
    there = {spot: index for index, spot in enumerate(spots)}
    swap = [(there[s], there[(s[0] ^ 7 * s[3],) + s[1:]]) for s in spots]

    def moved(array, r, other):
        pairs = []
        for z, y, xl, xh, c in spots:
            x = (2 * xh + xl + r) % 4
            pairs.append((there[z, y, xl, xh, c], there[z, y, x % 2, x // 2, c ^ other]))
        return lax.ppermute(array, ALL, pairs) if r or other else array

    blk, pix = lax.axis_index("blk"), lax.axis_index("pix")
    z, x_hi = blk >> 3, pix >> 1
    place = jnp.stack([pix & 1, x_hi, z >> 2, 2 * x_hi + (blk & 1)]).astype(jnp.int32)
    sds = jax.ShapeDtypeStruct
    n_col, chips = len(column[0]), 4
    count = n_blk * owned
    groups = n_col // PACK
    held = n_col * CAP

    raw = lax.ppermute(bundles.transpose(0, 2, 1), ALL, swap)
    *sends, code = call(
        slots_kernel,
        place,
        [assign.reshape(1, rows), pixels.T],
        (sds((2, held, LANES), bf16),) * chips + (sds((1, rows), jnp.int32),),
        [vmem((LANES, rows), bf16), vmem((1, rows), f32)],
        16,
    )
    copies = call(
        spread_kernel, place, [raw], sds((n_col, width, LANES), bf16), [vmem((width, LANES), bf16)], 4, [sends[0]]
    )
    gathered = exchanged(copies, column)
    received = [moved(send, r, 0) for r, send in enumerate(sends)]
    theirs = moved(call(stack_kernel, None, received, sds((chips, held, LANES), bf16), [], 8), 0, 1)

    below = groups * CAP
    slots = 2 * chips * CAP
    scale = bands * rows * n_pix / count
    square = sds((groups, LANES, LANES), bf16)
    grams = call(
        gram_kernel,
        None,
        [gathered],
        (square, square, sds((groups, LANES), f32)),
        [vmem((groups, LANES), f32)],
        16,
    )
    solved = call(
        lambda *refs: solve_kernel(*refs, scale=scale),
        place,
        [gathered, *grams, theirs, *received],
        (sds((chips, below + 8, LANES), f32),) * 2,
        [
            vmem((groups, slots, LANES), f32),
            vmem((groups, slots, LANES), f32),
            vmem((2, count, LANES), f32),
        ],
        16,
    )
    mine, others = solved[0], moved(solved[1], 0, 1)
    back = [moved(jnp.stack([mine[r], others[r]]), -r, 0) for r in range(1, chips)]
    outs = (sds((width, rows), f32), sds((1, count), f32))
    chosen, energy = call(return_kernel, None, [code, mine, others, *back], outs, [], 16)
    return chosen.T, energy


def solution(mesh):
    placed = (P(("blk", "pix"), None), P("blk", None, None), P(("blk", "pix"), None))
    return jax.shard_map(
        per_device,
        mesh=mesh,
        in_specs=placed,
        out_specs=(P(("blk", "pix"), None), P("blk", None)),
        check_vma=False,
    )
```

```python
import jax
import jax.numpy as jnp
from jax import lax
from jax.experimental import pallas as pl
from jax.experimental.pallas import tpu as pltpu
from jax.sharding import PartitionSpec as P

ITERS = 8
CAP = 16
LANES = 256
ROOT = 0.125
PACK = 4
ALL = ("blk", "pix")
f32, bf16 = jnp.float32, jnp.bfloat16


def iota(shape, dim):
    return lax.broadcasted_iota(jnp.int32, shape, dim)


def one_hot(where):
    return where.astype(f32).astype(bf16)


def split(x):
    high = x.astype(bf16)
    return high, (x - high.astype(f32)).astype(bf16)


def dot(a, b):
    return jnp.dot(a, b, preferred_element_type=f32)


def dot_nt(a, b):
    return lax.dot_general(a, b, (((1,), (1,)), ((), ())), preferred_element_type=f32)


def prep_kernel(place, bundles, *rest):
    out = rest[-1]
    bands = bundles.shape[2]
    out[...] = jnp.where(iota(out.shape, 1) == bands, ROOT, 0.0).astype(bf16)
    out[:, :bands] = bundles[place[0]]


def slots_kernel(place, labels, pixels, send, code, wide, ranks):
    bands, rows = pixels.shape
    count = rows // (CAP // 2)
    wide[:bands] = pixels[...]
    wide[bands:] = jnp.where(iota((LANES - bands, rows), 0) == 0, ROOT, 0.0).astype(bf16)
    label = labels[...]
    chunk = 256
    upper = one_hot(iota((chunk, chunk), 0) <= iota((chunk, chunk), 1))
    carry = jnp.zeros((count, 1), f32)
    for q in range(rows // chunk):
        part = slice(q * chunk, (q + 1) * chunk)
        named = (iota((count, chunk), 0) == label[:, part]).astype(f32)
        running = dot(named.astype(bf16), upper) + carry
        ranks[:, part] = jnp.sum(named * running, axis=0, keepdims=True) - 1.0
        carry = running[:, chunk - 1 :]
    rank = ranks[...].astype(jnp.int32)
    other = (label >> 6) ^ (place[2] >> 2)
    handler = (label >> 1 & 1) * 4 + other * 2 + (label + place[0] & 1)
    local = (place[2] - ((label >> 4) ^ other * 3) & 3) * PACK + (place[4] - (label >> 2) & 3)
    slot = local * CAP + rank
    chips, _, held = send.shape[:3]
    for d in range(2 * chips):
        key = jnp.where(handler == d, slot, -1)
        send[d // 2, d % 2] = dot_nt(one_hot(iota((held, rows), 0) == key), wide[...]).astype(bf16)
    table_row = handler * (held // PACK) + (local >> 2) * CAP + rank
    code[...] = (local & 3) * 1024 + table_row


def stack_kernel(received, *rest):
    out = rest[-1]
    for j in range(out.shape[0]):
        out[j] = received[j, 1]


def blocks():
    return iota((1, LANES), 1) // (LANES // PACK)


def basis_of(bundles, g):
    return jnp.concatenate([b[g] for b in bundles], axis=0)


def gram_kernel(*refs):
    bundles, (high, low, steps, sums) = refs[:-4], refs[-4:]
    groups = high.shape[0]
    wide = LANES // PACK
    block = blocks()
    same = iota((LANES, LANES), 0) // wide == iota((LANES, LANES), 1) // wide
    for g in range(groups):
        basis = basis_of(bundles, g)
        gram = jnp.where(same, dot_nt(basis, basis), 0.0)
        sums[g : g + 1] = jnp.sum(jnp.abs(gram), axis=0, keepdims=True)
        high[g], low[g] = split(gram)
    total = sums[...]
    largest = jnp.zeros_like(total)
    for i in range(PACK):
        inside = block == i
        largest = jnp.where(inside, jnp.max(jnp.where(inside, total, 0.0), axis=1, keepdims=True), largest)
    steps[...] = 1.0 / largest


def solve_kernel(place, *refs, scale):
    bundles, (high, low, steps, received, theirs, mine_out, theirs_out, goal, state, parts) = refs[:-10], refs[-10:]
    sources = [s for j in range(theirs.shape[0]) for s in (received.at[j, 0], theirs.at[j])]
    outs = (mine_out, theirs_out)
    groups = state.shape[0]
    slots = len(sources) * CAP
    block = blocks()

    def pixels_of(local):
        return jnp.concatenate([s[local * CAP : (local + 1) * CAP] for s in sources], axis=0)

    for g in range(groups):
        found = dot_nt(jnp.concatenate([pixels_of(PACK * g + i) for i in range(PACK)], axis=0), basis_of(bundles, g))
        aim = found[:slots]
        for i in range(1, PACK):
            aim = jnp.where(block == i, found[i * slots : (i + 1) * slots], aim)
        goal[g] = aim
    for g in range(groups):
        state[g] = jnp.maximum(steps[g : g + 1] * goal[g], 0.0)

    def sweep(index, carry):
        for g in range(groups):
            a = state[g]
            first, second = split(a)
            both = dot(jnp.concatenate([first, second], axis=0), high[g])
            grad = both[:slots] + both[slots:] + dot(first, low[g])
            state[g] = jnp.maximum(a - steps[g : g + 1] * (grad - goal[g]), 0.0)
        return carry

    lax.fori_loop(1, ITERS, sweep, 0, unroll=True)
    parts[...] = jnp.zeros(parts.shape, f32)
    for g in range(groups):
        a = state[g]
        for s in range(len(sources)):
            outs[s % 2][s // 2, g * CAP : (g + 1) * CAP] = a[s * CAP : (s + 1) * CAP]
        spread = jnp.concatenate([jnp.where(block == i, a, 0.0) for i in range(PACK)], axis=0)
        both = dot(jnp.concatenate(split(spread), axis=0), basis_of(bundles, g))
        fitted = both[: PACK * slots] + both[PACK * slots :]
        for i in range(PACK):
            misfit = pixels_of(PACK * g + i).astype(f32) - fitted[i * slots : (i + 1) * slots]
            square = misfit * misfit
            z, y = (place[2] & 4) + (place[2] - g & 3) ^ 7 * place[1], place[4] - i & 3
            bundle = 16 * z + 4 * y + 2 * place[3] + place[0]
            for half in range(2):
                rows = slice(half * slots // 2, (half + 1) * slots // 2)
                parts[half, pl.ds(bundle, 1), :] = jnp.sum(square[rows], axis=0, keepdims=True)
    bands = LANES - 32
    below = groups * CAP
    for half in range(2):
        lines = parts[half].T
        lines = jnp.where(iota(lines.shape, 0) < bands, lines, 0.0)
        energy = jnp.sum(lines, axis=0, keepdims=True) / scale
        energy = jnp.concatenate([energy, jnp.zeros_like(energy)], axis=1)
        for j in (2 * half, 2 * half + 1):
            for i in range(2):
                outs[i][j, below:] = jnp.broadcast_to(energy, (8, LANES))


def return_kernel(code, back, chosen, energy):
    rows = code.shape[1]
    held, lanes = back.shape[2] - 8, back.shape[3]
    tables = [back.at[j, i] for j in range(back.shape[0]) for i in range(2)]
    handlers = len(tables)
    wide = lanes // PACK
    codes = code[...]
    pick = one_hot(iota((handlers * held, rows), 0) == codes & 1023)
    table = jnp.concatenate([t[:held] for t in tables], axis=0).T
    found = dot(jnp.concatenate(split(table), axis=0), pick)
    found = found[:lanes] + found[lanes:]
    which = codes >> 10
    result = found[:wide]
    for i in range(1, PACK):
        result = jnp.where(which == i, found[i * wide : (i + 1) * wide], result)
    chosen[...] = result
    total = tables[0][held : held + 1]
    for t in tables[1:]:
        total = total + t[held : held + 1]
    energy[...] = total[:, : energy.shape[1]]


def vmem(shape, dtype):
    return pltpu.VMEM(shape, dtype)


def call(kernel, place, args, outs, scratch, limit, after=()):
    spec = pl.BlockSpec(memory_space=pltpu.VMEM)
    head = [] if place is None else [place]
    return pl.pallas_call(
        kernel,
        out_shape=outs,
        in_specs=[pl.BlockSpec(memory_space=pltpu.SMEM)] * len(head) + [spec] * len(args) + [pl.BlockSpec(memory_space=pl.ANY)] * len(after),
        out_specs=jax.tree.map(lambda _: spec, outs),
        scratch_shapes=scratch,
        compiler_params=pltpu.CompilerParams(vmem_limit_bytes=limit << 20),
    )(*head, *args, *after)


def spots_of(n_blk, n_pix):
    return [(b // 8, b // 2 % 4, b % 2, p // 2, p % 2) for b in range(n_blk) for p in range(n_pix)]


def grouped(spots, key):
    groups = {}
    for index, spot in enumerate(spots):
        groups.setdefault(key(*spot), []).append(index)
    return list(groups.values())


def exchanged(array, groups):
    return lax.all_to_all(array, ALL, 0, 0, tiled=True, axis_index_groups=groups)


def per_device(pixels, bundles, assign):
    rows, bands = pixels.shape
    owned, _, width = bundles.shape
    n_blk, n_pix = lax.axis_size("blk"), lax.axis_size("pix")
    spots = spots_of(n_blk, n_pix)
    there = {spot: index for index, spot in enumerate(spots)}

    def sent(array, target):
        return lax.ppermute(array, ALL, [(there[s], there[target(*s)]) for s in spots])

    row = grouped(spots, lambda z, y, xl, xh, c: (z, y, c))

    def to_sibling(array):
        return sent(array, lambda z, y, xl, xh, c: (z, y, xl, xh, c ^ 1))

    blk, pix = lax.axis_index("blk"), lax.axis_index("pix")
    z, x_hi = blk >> 3, pix >> 1
    place = jnp.stack([pix & 1, x_hi, z, blk & 1, blk >> 1 & 3]).astype(jnp.int32)
    sds = jax.ShapeDtypeStruct
    chips = len(row[0])
    count = n_blk * owned
    groups = 4
    held = groups * PACK * CAP

    send, code = call(
        slots_kernel,
        place,
        [assign.reshape(1, rows), pixels.T],
        (sds((chips, 2, held, LANES), bf16), sds((1, rows), jnp.int32)),
        [vmem((LANES, rows), bf16), vmem((1, rows), f32)],
        16,
    )
    basis = call(prep_kernel, place, [bundles.transpose(0, 2, 1)], sds((width, LANES), bf16), [], 4, [send])
    pieces = []
    for q in range(groups):

        def around(z, y, xl, xh, c):
            held = z ^ 7 * xh
            return held & 4 | held + q & 3, y, xl, xh, c

        pieces.append(sent(basis, around))
    levels = jnp.stack(pieces)
    gathered = [levels]
    for r in range(1, PACK):
        gathered.append(sent(levels, lambda z, y, xl, xh, c: (z, y + r & 3, xl, xh, c)))
    received = exchanged(send, row)
    theirs = to_sibling(call(stack_kernel, None, [received], sds((chips, held, LANES), bf16), [], 8, gathered[1:]))

    below = groups * CAP
    slots = 2 * chips * CAP
    scale = bands * rows * n_pix / count
    square = sds((groups, LANES, LANES), bf16)
    grams = call(
        gram_kernel,
        None,
        gathered,
        (square, square, sds((groups, LANES), f32)),
        [vmem((groups, LANES), f32)],
        16,
    )
    solved = call(
        lambda *refs: solve_kernel(*refs, scale=scale),
        place,
        [*gathered, *grams, received, theirs],
        (sds((chips, below + 8, LANES), f32),) * 2,
        [
            vmem((groups, slots, LANES), f32),
            vmem((groups, slots, LANES), f32),
            vmem((2, count, LANES), f32),
        ],
        16,
    )
    back = exchanged(jnp.stack([solved[0], to_sibling(solved[1])], axis=1), row)
    outs = (sds((width, rows), f32), sds((1, count), f32))
    chosen, energy = call(return_kernel, None, [code, back], outs, [], 16)
    return chosen.T, energy


def solution(mesh):
    placed = (P(("blk", "pix"), None), P("blk", None, None), P(("blk", "pix"), None))
    return jax.shard_map(
        per_device,
        mesh=mesh,
        in_specs=placed,
        out_specs=(P(("blk", "pix"), None), P("blk", None)),
        check_vma=False,
    )
```

```python
import jax
import jax.numpy as jnp
from jax import lax
from jax.experimental import pallas as pl
from jax.experimental.pallas import tpu as pltpu
from jax.sharding import PartitionSpec as P

ITERS = 8
CAP = 16
LANES = 256
ROOT = 0.125
PACK = 4
ALL = ("blk", "pix")
f32, bf16 = jnp.float32, jnp.bfloat16


def iota(shape, dim):
    return lax.broadcasted_iota(jnp.int32, shape, dim)


def one_hot(where):
    return where.astype(f32).astype(bf16)


def split(x):
    high = x.astype(bf16)
    return high, (x - high.astype(f32)).astype(bf16)


def dot(a, b):
    return jnp.dot(a, b, preferred_element_type=f32)


def dot_nt(a, b):
    return lax.dot_general(a, b, (((1,), (1,)), ((), ())), preferred_element_type=f32)


def spread_kernel(place, bundles, *rest):
    out, wide = rest[-2:]
    bands = bundles.shape[2]
    wide[...] = jnp.where(iota(wide.shape, 1) == bands, ROOT, 0.0).astype(bf16)
    wide[:, :bands] = bundles[place[0]]
    for i in range(out.shape[0]):
        out[i] = wide[...]


def slots_kernel(place, labels, pixels, *rest):
    outs, (code, wide, ranks) = rest[:-3], rest[-3:]
    bands, rows = pixels.shape
    count = rows // (CAP // 2)
    wide[:bands] = pixels[...]
    wide[bands:] = jnp.where(iota((LANES - bands, rows), 0) == 0, ROOT, 0.0).astype(bf16)
    label = labels[...]
    chunk = 256
    upper = one_hot(iota((chunk, chunk), 0) <= iota((chunk, chunk), 1))
    carry = jnp.zeros((count, 1), f32)
    for q in range(rows // chunk):
        part = slice(q * chunk, (q + 1) * chunk)
        named = (iota((count, chunk), 0) == label[:, part]).astype(f32)
        running = dot(named.astype(bf16), upper) + carry
        ranks[:, part] = jnp.sum(named * running, axis=0, keepdims=True) - 1.0
        carry = running[:, chunk - 1 :]
    rank = ranks[...].astype(jnp.int32)
    other = (label >> 6) ^ place[2]
    chip = other * 2 + (label >> 1 & 1)
    handler = (chip - place[3] & 3) * 2 + (label + place[0] & 1)
    local = ((label >> 4 & 3) ^ other * 3) * PACK + (label >> 2 & 3)
    slot = local * CAP + rank
    held = outs[0].shape[1]
    for d in range(2 * len(outs)):
        key = jnp.where(handler == d, slot, -1)
        outs[d // 2][d % 2] = dot_nt(one_hot(iota((held, rows), 0) == key), wide[...]).astype(bf16)
    table_row = handler * (held // PACK) + (local >> 2) * CAP + rank
    code[...] = (local & 3) * 1024 + table_row


def stack_kernel(*refs):
    for r, m in enumerate(refs[:-1]):
        refs[-1][r] = m[1]


def blocks():
    return iota((1, LANES), 1) // (LANES // PACK)


def basis_of(bundles, g):
    return jnp.concatenate([bundles[PACK * g + i] for i in range(PACK)], axis=0)


def gram_kernel(bundles, high, low, steps, sums):
    groups = high.shape[0]
    wide = LANES // PACK
    block = blocks()
    same = iota((LANES, LANES), 0) // wide == iota((LANES, LANES), 1) // wide
    for g in range(groups):
        basis = basis_of(bundles, g)
        gram = jnp.where(same, dot_nt(basis, basis), 0.0)
        sums[g : g + 1] = jnp.sum(jnp.abs(gram), axis=0, keepdims=True)
        high[g], low[g] = split(gram)
    total = sums[...]
    largest = jnp.zeros_like(total)
    for i in range(PACK):
        inside = block == i
        largest = jnp.where(inside, jnp.max(jnp.where(inside, total, 0.0), axis=1, keepdims=True), largest)
    steps[...] = 1.0 / largest


def solve_kernel(place, bundles, high, low, steps, theirs, *rest, scale):
    sources = [s for r, m in enumerate(rest[:-5]) for s in (m.at[0], theirs.at[r])]
    outs = rest[-5:-3]
    goal, state, parts = rest[-3:]
    groups = state.shape[0]
    slots = len(sources) * CAP
    block = blocks()

    def pixels_of(local):
        return jnp.concatenate([s[local * CAP : (local + 1) * CAP] for s in sources], axis=0)

    for g in range(groups):
        found = dot_nt(jnp.concatenate([pixels_of(PACK * g + i) for i in range(PACK)], axis=0), basis_of(bundles, g))
        aim = found[:slots]
        for i in range(1, PACK):
            aim = jnp.where(block == i, found[i * slots : (i + 1) * slots], aim)
        goal[g] = aim
    for g in range(groups):
        state[g] = jnp.maximum(steps[g : g + 1] * goal[g], 0.0)

    def sweep(index, carry):
        for g in range(groups):
            a = state[g]
            first, second = split(a)
            both = dot(jnp.concatenate([first, second], axis=0), high[g])
            grad = both[:slots] + both[slots:] + dot(first, low[g])
            state[g] = jnp.maximum(a - steps[g : g + 1] * (grad - goal[g]), 0.0)
        return carry

    lax.fori_loop(1, ITERS, sweep, 0, unroll=True)
    parts[...] = jnp.zeros(parts.shape, f32)
    for g in range(groups):
        a = state[g]
        for s in range(len(sources)):
            outs[s % 2][s // 2, g * CAP : (g + 1) * CAP] = a[s * CAP : (s + 1) * CAP]
        spread = jnp.concatenate([jnp.where(block == i, a, 0.0) for i in range(PACK)], axis=0)
        both = dot(jnp.concatenate(split(spread), axis=0), basis_of(bundles, g))
        fitted = both[: PACK * slots] + both[PACK * slots :]
        for i in range(PACK):
            misfit = pixels_of(PACK * g + i).astype(f32) - fitted[i * slots : (i + 1) * slots]
            square = misfit * misfit
            bundle = 16 * (4 * place[2] + g ^ 7 * place[1]) + 4 * i + 2 * (place[3] & 1) + place[0]
            for half in range(2):
                both = square[2 * half * CAP : 2 * (half + 1) * CAP]
                both = both + square[2 * (half + 2) * CAP : 2 * (half + 3) * CAP]
                parts[half, pl.ds(bundle, 1), :] = jnp.sum(both, axis=0, keepdims=True)
    bands = LANES - 32
    below = groups * CAP
    for half in range(2):
        lines = parts[half].T
        lines = jnp.where(iota(lines.shape, 0) < bands, lines, 0.0)
        energy = jnp.sum(lines, axis=0, keepdims=True) / scale
        energy = jnp.concatenate([energy, jnp.zeros_like(energy)], axis=1)
        for r in (half, half + 2):
            for i in range(2):
                outs[i][r, below:] = jnp.broadcast_to(energy, (8, LANES))


def pick_kernel(code, *rest):
    pick = rest[-1]
    pick[...] = one_hot(iota(pick.shape, 0) == code[...] & 1023)


def return_kernel(code, pick, mine, theirs, back1, back2, back3, chosen, energy):
    rows = code.shape[1]
    held, lanes = mine.shape[1] - 8, mine.shape[2]
    backs = (back1, back2, back3)
    tables = [mine.at[0], theirs.at[0]] + [b.at[i] for b in backs for i in range(2)]
    wide = lanes // PACK
    codes = code[...]
    table = jnp.concatenate([t[:held] for t in tables], axis=0).T
    found = dot(jnp.concatenate(split(table), axis=0), pick[...])
    found = found[:lanes] + found[lanes:]
    which = codes >> 10
    result = found[:wide]
    for i in range(1, PACK):
        result = jnp.where(which == i, found[i * wide : (i + 1) * wide], result)
    chosen[...] = result
    total = tables[0][held : held + 1]
    for t in tables[1:]:
        total = total + t[held : held + 1]
    energy[...] = total[:, : energy.shape[1]]


def vmem(shape, dtype):
    return pltpu.VMEM(shape, dtype)


def call(kernel, place, args, outs, scratch, limit, after=()):
    spec = pl.BlockSpec(memory_space=pltpu.VMEM)
    head = [] if place is None else [place]
    return pl.pallas_call(
        kernel,
        out_shape=outs,
        in_specs=[pl.BlockSpec(memory_space=pltpu.SMEM)] * len(head) + [spec] * len(args) + [pl.BlockSpec(memory_space=pl.ANY)] * len(after),
        out_specs=jax.tree.map(lambda _: spec, outs),
        scratch_shapes=scratch,
        compiler_params=pltpu.CompilerParams(vmem_limit_bytes=limit << 20),
    )(*head, *args, *after)


def spots_of(n_blk, n_pix):
    return [(b // 8, b // 2 % 4, b % 2, p // 2, p % 2) for b in range(n_blk) for p in range(n_pix)]


def grouped(spots, key):
    groups = {}
    for index, spot in enumerate(spots):
        groups.setdefault(key(*spot), []).append(index)
    return list(groups.values())


def exchanged(array, groups):
    return lax.all_to_all(array, ALL, 0, 0, tiled=True, axis_index_groups=groups)


def per_device(pixels, bundles, assign):
    rows, bands = pixels.shape
    owned, _, width = bundles.shape
    n_blk, n_pix = lax.axis_size("blk"), lax.axis_size("pix")
    spots = spots_of(n_blk, n_pix)
    column = grouped(spots, lambda z, y, xl, xh, c: (z // 4, xl, xh, c))
    there = {spot: index for index, spot in enumerate(spots)}
    swap = [(there[s], there[(s[0] ^ 7 * s[3],) + s[1:]]) for s in spots]

    def moved(array, r, other):
        pairs = []
        for z, y, xl, xh, c in spots:
            x = (2 * xh + xl + r) % 4
            pairs.append((there[z, y, xl, xh, c], there[z, y, x % 2, x // 2, c ^ other]))
        return lax.ppermute(array, ALL, pairs) if r or other else array

    blk, pix = lax.axis_index("blk"), lax.axis_index("pix")
    z, x_hi = blk >> 3, pix >> 1
    place = jnp.stack([pix & 1, x_hi, z >> 2, 2 * x_hi + (blk & 1)]).astype(jnp.int32)
    sds = jax.ShapeDtypeStruct
    n_col, chips = len(column[0]), 4
    count = n_blk * owned
    groups = n_col // PACK
    held = n_col * CAP

    raw = lax.ppermute(bundles.transpose(0, 2, 1), ALL, swap)
    *sends, code = call(
        slots_kernel,
        place,
        [assign.reshape(1, rows), pixels.T],
        (sds((2, held, LANES), bf16),) * chips + (sds((1, rows), jnp.int32),),
        [vmem((LANES, rows), bf16), vmem((1, rows), f32)],
        16,
    )
    copies = call(
        spread_kernel, place, [raw], sds((n_col, width, LANES), bf16), [vmem((width, LANES), bf16)], 4, [sends[0]]
    )
    gathered = exchanged(copies, column)
    received = [moved(send, r, 0) for r, send in enumerate(sends)]
    theirs = moved(call(stack_kernel, None, received, sds((chips, held, LANES), bf16), [], 8), 0, 1)

    below = groups * CAP
    slots = 2 * chips * CAP
    scale = bands * rows * n_pix / count
    square = sds((groups, LANES, LANES), bf16)
    grams = call(
        gram_kernel,
        None,
        [gathered],
        (square, square, sds((groups, LANES), f32)),
        [vmem((groups, LANES), f32)],
        16,
    )
    solved = call(
        lambda *refs: solve_kernel(*refs, scale=scale),
        place,
        [gathered, *grams, theirs, *received],
        (sds((chips, below + 8, LANES), f32),) * 2,
        [
            vmem((groups, slots, LANES), f32),
            vmem((groups, slots, LANES), f32),
            vmem((2, count, LANES), f32),
        ],
        16,
    )
    mine, others = solved[0], moved(solved[1], 0, 1)
    back = [moved(jnp.stack([mine[r], others[r]]), -r, 0) for r in range(1, chips)]
    pick = call(pick_kernel, None, [code], sds((2 * chips * below, rows), bf16), [], 8, [solved[0]])
    outs = (sds((width, rows), f32), sds((1, count), f32))
    chosen, energy = call(return_kernel, None, [code, pick, mine, others, *back], outs, [], 16)
    return chosen.T, energy


def solution(mesh):
    placed = (P(("blk", "pix"), None), P("blk", None, None), P(("blk", "pix"), None))
    return jax.shard_map(
        per_device,
        mesh=mesh,
        in_specs=placed,
        out_specs=(P(("blk", "pix"), None), P("blk", None)),
        check_vma=False,
    )
```
